32 devices in a mesh: groups: 2 (over x), planes: 4 (over y, core), chan: 4 (over z).
Axes of the slice: x: 2, y: 2, z: 4, core: 2. Of those that a mesh axis runs over, the one named last changes fastest.
Arguments:
- field: float32 [2, 16, 128, 128, 128], P('groups', None, ('planes', 'chan')), parts along dimension 0, may hold values from -6 to 6
- cotangent: float32 [2, 16, 128, 128, 128], P('groups', None, ('planes', 'chan')), parts along dimension 0, may hold values from -6 to 6
- spec_weight: float32 [2, 16, 16, 64, 2048], P(None, None, None, 'planes', 'chan'), may hold values from -1.5 to 1.5
- point_weight: float32 [16, 16], replicated, may hold values from -1.5 to 1.5
- bias: float32 [16], replicated, may hold values from -3 to 3
Outputs:
- output: float32 [2, 16, 128, 128, 128], P('groups', None, ('planes', 'chan')), parts along dimension 0
- field_grad: float32 [2, 16, 128, 128, 128], P('groups', None, ('planes', 'chan')), parts along dimension 0
- weight_grad: float32 [4, 16, 16, 64, 2048], P('groups', None, None, 'planes', 'chan'), parts along dimension 0
The draws below stay inside these ranges and needn't reach their ends.
There are 2 independent parts, one for each index of `groups`. The reference program is written for one: setup_inputs(seed, part) draws one part's arguments, and reference() takes and returns one part's arrays. A program takes and returns all parts, laid end to end along the dimension named above; an argument that names none is the same for every part. Nothing has to cross between parts.
All inputs are finite; a program needn't handle non-finite values.
Results may differ from the reference program's by a relative error of at most 0.0001.
Values sent between devices are 32-bit elements; how exact they have to be, the bound alone decides.
No kernel may reach another device: no remote copies, remote signals or barrier semaphores. Data moves between devices by JAX's collectives and lax.ppermute only.
A program may use at most 192 MiB of HBM per device.

```python
import jax
import jax.numpy as jnp
from jax import lax

CH = 16
GX = 128
GY = 128
GZ = 128
MODES = 32
BATCH = 1


def steps_of(rng, extent, cuts, low, high):
    def one(position, blocks):
        draws = jax.random.uniform(jax.random.fold_in(jax.random.fold_in(rng, 6), position), (blocks,), jnp.float32, low / len(cuts), high / len(cuts))
        return jnp.repeat(jnp.exp(draws), extent[position] // blocks).reshape((-1,) + (1,) * (len(extent) - position - 1))

    loudness = one(*cuts[0])
    for cut in cuts[1:]:
        loudness = loudness * one(*cut)
    return loudness


def normal_values(rng, dims, width, reach, shards=(), kind=jnp.bfloat16):
    gain = steps_of(rng, dims, shards, -0.22, 0.18) if shards else 1.0
    values = jax.random.normal(rng, dims, jnp.float32) * width * gain
    return jnp.minimum(jnp.maximum(values, -reach), reach).astype(kind)


def setup_inputs(seed: int = 0, part: int = 0) -> dict:
    keys = jax.random.split(jax.random.key(seed), 6)
    own_keys = jax.random.split(jax.random.fold_in(keys[5], part), 6)
    return {
        "field": normal_values(own_keys[0], (BATCH, CH, GX, GY, GZ), 1.0, 6.0, ((2, 16),), jnp.float32),
        "cotangent": normal_values(own_keys[1], (BATCH, CH, GX, GY, GZ), 1.0, 6.0, ((2, 16),), jnp.float32),
        "spec_weight": normal_values(keys[2], (2, CH, CH, 2 * MODES, 2 * MODES * MODES), CH ** -0.5, 1.5, ((3, 4), (4, 4)), jnp.float32),
        "point_weight": normal_values(keys[3], (CH, CH), CH ** -0.5, 1.5, (), jnp.float32),
        "bias": normal_values(keys[4], (CH,), 0.5, 3.0, (), jnp.float32),
    }


def retained_index(length):
    return jnp.concatenate([jnp.arange(MODES), jnp.arange(length - MODES, length)])

def layer(field_value, weight_value, point_weight, bias):
    first_modes = retained_index(GX)
    second_modes = retained_index(GY)
    transform = jnp.fft.rfftn(field_value, axes=(2, 3, 4))
    transform = jnp.take(transform, first_modes, axis=2)
    transform = jnp.take(transform, second_modes, axis=3)
    transform = transform[..., :MODES]
    spec_re = jnp.real(transform)
    spec_im = jnp.imag(transform)
    shaped = weight_value.reshape(2, CH, CH, 2 * MODES, 2 * MODES, MODES)
    weight_re = shaped[0]
    weight_im = shaped[1]

    def contract(operand, weights):
        return jnp.einsum('bifkm,iokfm->bofkm', operand, weights, precision=lax.Precision.HIGHEST)
    mixed_re = contract(spec_re, weight_re) - contract(spec_im, weight_im)
    mixed_im = contract(spec_re, weight_im) + contract(spec_im, weight_re)
    mixed_modes = lax.complex(mixed_re, mixed_im)
    filled = jnp.zeros((BATCH, CH, GX, GY, GZ // 2 + 1), dtype=mixed_modes.dtype)
    filled = filled.at[:, :, first_modes[:, None], second_modes[None, :], :MODES].set(mixed_modes)
    spectral = jnp.fft.irfftn(filled, s=(GX, GY, GZ), axes=(2, 3, 4))
    pointwise = jnp.einsum('bixyz,io->boxyz', field_value, point_weight, precision=lax.Precision.HIGHEST)
    preactivation = spectral + pointwise + bias[None, :, None, None, None]
    return jax.nn.gelu(preactivation, approximate=False)

def reference(field, cotangent, spec_weight, point_weight, bias):

    def closed(field_value, weight_value):
        return layer(field_value, weight_value, point_weight, bias)
    output, pullback = jax.vjp(closed, field, spec_weight)
    field_grad, weight_grad = pullback(cotangent)
    return (output, field_grad, weight_grad)
```

```python
import functools
import math

import numpy as np

import jax
import jax.numpy as jnp
from jax import lax
from jax.experimental import pallas as pl
from jax.experimental.pallas import tpu as pltpu
from jax.sharding import PartitionSpec as P


exact_mode = lax.Precision.HIGHEST


def retained(s, length):
    indices = jnp.arange(2 * s.modes)
    return jnp.where(indices < s.modes, indices, length - 2 * s.modes + indices)


def phase_table(positions, freqs, length):
    turn_count = positions[:, None] * freqs[None, :] % length
    angles = turn_count.astype(jnp.float32) * (2.0 * math.pi / length)
    return (jnp.cos(angles), jnp.sin(angles))


def plain_analysis(s, field):
    batch_size, channels, local_planes, second_length, third_length = field.shape
    plane_count = lax.axis_size("planes")
    channel_groups = lax.axis_size("chan")
    group_width = channels // channel_groups
    local_modes = 2 * s.modes // plane_count
    first_length = local_planes * plane_count * channel_groups
    cosine, sine_part = phase_table(
        jnp.arange(second_length), retained(s, second_length), second_length
    )
    second_table = jnp.stack([cosine, -sine_part], 1).reshape(
        second_length, 2, plane_count, local_modes
    )
    cosine, sine_part = phase_table(jnp.arange(third_length), jnp.arange(s.modes), third_length)
    third_table = jnp.stack(
        [jnp.stack([cosine, -sine_part], 1), jnp.stack([sine_part, cosine], 1)], 0
    )
    grouped = field.reshape(
        batch_size, channel_groups, group_width, local_planes, second_length, third_length
    )
    second_pass = jnp.einsum("bcdxyz,yspk->bcdxspkz", grouped, second_table, precision=exact_mode)
    spectra = jnp.einsum("bcdxspkz,sztm->bpckxdtm", second_pass, third_table, precision=exact_mode)
    spectra = spectra.reshape(
        batch_size, plane_count * channel_groups, local_modes, local_planes, group_width * 2 * s.modes
    )
    arrived = lax.all_to_all(spectra, ("planes", "chan"), split_axis=1, concat_axis=3, tiled=True)
    positions = jnp.arange(first_length)
    arrived = arrived.reshape(batch_size, local_modes, first_length, group_width, 2, s.modes)
    cosine, sine_part = phase_table(positions, retained(s, first_length), first_length)
    first_table = jnp.stack(
        [jnp.stack([cosine, -sine_part], 1), jnp.stack([sine_part, cosine], 1)], 1
    )
    first_pass = jnp.einsum("bkxdsm,xstf->bkdtfm", arrived, first_table, precision=exact_mode)
    first_pass = first_pass.reshape(batch_size, local_modes, group_width, 2, 2 * s.modes * s.modes)
    return lax.all_to_all(first_pass, "chan", split_axis=4, concat_axis=2, tiled=True)


def plain_synthesis(s, spectrum):
    batch_size, local_modes, channels = (spectrum.shape[0], spectrum.shape[1], spectrum.shape[2])
    plane_count = lax.axis_size("planes")
    channel_groups = lax.axis_size("chan")
    group_width = channels // channel_groups
    local_planes = s.gx // (plane_count * channel_groups)
    gathered = lax.all_to_all(spectrum, "chan", split_axis=2, concat_axis=4, tiled=True)
    gathered = gathered.reshape(batch_size, local_modes, group_width, 2, 2 * s.modes, s.modes)
    cosine, sine_part = phase_table(jnp.arange(s.gx), retained(s, s.gx), s.gx)
    cosine_t = cosine.T
    sine_t = sine_part.T
    first_inverse = jnp.stack(
        [jnp.stack([cosine_t, sine_t], -1), jnp.stack([-sine_t, cosine_t], -1)], 0
    )
    first_pass = jnp.einsum("bkdsfm,sfxt->bkxdtm", gathered, first_inverse, precision=exact_mode)
    first_pass = first_pass.reshape(batch_size, local_modes, s.gx, group_width * 2 * s.modes)
    returned = lax.all_to_all(
        first_pass[:, None], ("planes", "chan"), split_axis=3, concat_axis=1, tiled=True
    )
    returned = returned.reshape(
        batch_size, plane_count, channel_groups, local_modes, local_planes, group_width, 2, s.modes
    )
    source_form = "bpckxdtm"
    cosine, sine_part = phase_table(jnp.arange(s.gz), jnp.arange(s.modes), s.gz)
    cosine_t = cosine.T
    sine_t = sine_part.T
    third_inverse = jnp.stack(
        [jnp.stack([cosine_t, sine_t], 1), jnp.stack([-sine_t, cosine_t], 1)], 0
    )
    depth_pass = jnp.einsum(
        source_form + ",tmuz->bcdxpkuz", returned, third_inverse, precision=exact_mode
    )
    cosine, sine_part = phase_table(jnp.arange(s.gy), retained(s, s.gy), s.gy)
    second_inverse = jnp.stack([cosine.T, -sine_part.T], 0).reshape(2, plane_count, local_modes, s.gy)
    physical = jnp.einsum("bcdxpkuz,upky->bcdxyz", depth_pass, second_inverse, precision=exact_mode)
    return physical.reshape(batch_size, channels, local_planes, s.gy, s.gz)


def mode_weighting(s, mode_count):
    depth_mode = jnp.arange(mode_count) % s.modes
    return jnp.where(depth_mode == 0, 1.0, 2.0).astype(jnp.float32) / float(s.gx * s.gy * s.gz)


def contract(operand, weights):
    return jnp.einsum("bkin,iokn->bkon", operand, weights, precision=exact_mode)


def adjoint(operand, weights):
    return jnp.einsum("bkon,iokn->bkin", operand, weights, precision=exact_mode)


def outer_sum(first_operand, second_operand):
    return jnp.einsum("bkin,bkon->iokn", first_operand, second_operand, precision=exact_mode)


def plain_local(s, field, cotangent, spec_weight, point_weight, bias):
    spectrum = plain_analysis(s, field)
    weight_re = spec_weight[0]
    weight_im = spec_weight[1]
    spec_re = spectrum[:, :, :, 0]
    spec_im = spectrum[:, :, :, 1]
    weighting = mode_weighting(s, spectrum.shape[-1])
    mixed_re = (contract(spec_re, weight_re) - contract(spec_im, weight_im)) * weighting
    mixed_im = (contract(spec_re, weight_im) + contract(spec_im, weight_re)) * weighting
    mixed_modes = jnp.stack([mixed_re, mixed_im], 3)
    spectral = plain_synthesis(s, mixed_modes)
    pointwise = jnp.einsum("bixyz,io->boxyz", field, point_weight, precision=exact_mode)
    preactivation = spectral + pointwise + bias[None, :, None, None, None]
    normal_cdf = 0.5 * (1.0 + lax.erf(preactivation * (1.0 / math.sqrt(2.0))))
    output = preactivation * normal_cdf
    derivative = normal_cdf + preactivation * jnp.exp(-0.5 * preactivation * preactivation) * (
        1.0 / math.sqrt(2.0 * math.pi)
    )
    pre_grad = cotangent * derivative
    raw_grad = plain_analysis(s, pre_grad)
    grad_re = raw_grad[:, :, :, 0] * weighting
    grad_im = raw_grad[:, :, :, 1] * weighting
    spectrum_grad = jnp.stack(
        [
            adjoint(grad_re, weight_re) + adjoint(grad_im, weight_im),
            adjoint(grad_im, weight_re) - adjoint(grad_re, weight_im),
        ],
        3,
    )
    weight_grad = jnp.stack(
        [
            outer_sum(spec_re, grad_re) + outer_sum(spec_im, grad_im),
            outer_sum(spec_re, grad_im) - outer_sum(spec_im, grad_re),
        ],
        0,
    )
    local_grad = jnp.einsum("boxyz,io->bixyz", pre_grad, point_weight, precision=exact_mode)
    field_grad = local_grad + plain_synthesis(s, spectrum_grad)
    return (output, field_grad, weight_grad)


LANES = 128
X_CHUNKS = 1
MODE_CHUNKS = 1
f32 = jnp.float32
bf16 = jnp.bfloat16


class Sizes:
    def __init__(self, field, spec_weight):
        self.planes = lax.axis_size("planes")
        self.chan = lax.axis_size("chan")
        self.owners = self.planes * self.chan
        _, self.ch, self.lx, self.gy, self.gz = field.shape
        self.gx = self.lx * self.owners
        _, _, _, self.jl, local_flat = spec_weight.shape
        self.jy = self.jl * self.planes
        self.flat = local_flat
        self.modes = self.jy // 2
        self.jxl = local_flat // self.modes
        self.jx = self.jxl * self.chan
        self.gw = self.ch // self.chan
        self.scale = 1.0 / float(self.gx * self.gy * self.gz)

    def fits(self):
        return (
            self.gw * self.modes == LANES
            and self.gz == LANES
            and self.gy == LANES
            and self.jy * 2 == LANES
            and self.jx * 2 == LANES
            and self.gw % 2 == 0
            and self.flat % LANES == 0
            and self.jl % (16 * MODE_CHUNKS) == 0
            and self.lx % (4 * X_CHUNKS) == 0
            and self.gx == 2 * LANES // 2
        )


def kept(count, length):
    index = np.arange(count)
    return np.where(index < count // 2, index, length - count + index)


def waves(freqs, length):
    turns = (freqs[:, None] * np.arange(length)[None, :]) % length
    angles = turns * (2.0 * math.pi / length)
    return np.cos(angles), np.sin(angles)


def two_terms(table):
    table = np.asarray(table, np.float32)
    high = table.astype(jnp.bfloat16)
    low = (table - high.astype(np.float32)).astype(jnp.bfloat16)
    return high, low


def stacked_square(table):
    high, low = two_terms(table)
    return np.concatenate([np.concatenate([high, high], 1), np.concatenate([low, low], 1)], 0)


def second_tables(s):
    cosine, sine = waves(kept(s.jy, s.gy), s.gy)
    forward = np.concatenate([cosine, -sine], 0)
    return stacked_square(forward), stacked_square(forward.T)


def third_tables(s):
    cosine, sine = waves(np.arange(s.modes), s.gz)
    base = np.zeros((s.gw, 2, s.gz, 2, s.gw, s.modes))
    for c in range(s.gw):
        base[c, 0, :, 0, c] = cosine.T
        base[c, 0, :, 1, c] = -sine.T
        base[c, 1, :, 0, c] = sine.T
        base[c, 1, :, 1, c] = cosine.T
    forward = base.reshape(s.gw * 2 * s.gz, 2 * LANES)
    inverse = np.zeros((s.gw, 2, s.gw, s.modes, 2, s.gz))
    for c in range(s.gw):
        inverse[c, 0, c, :, 0, :] = cosine
        inverse[c, 0, c, :, 1, :] = sine
        inverse[c, 1, c, :, 0, :] = -sine
        inverse[c, 1, c, :, 1, :] = cosine
    inverse = inverse.reshape(s.gw, 2 * LANES, 2 * s.gz)
    return two_terms(forward) + two_terms(inverse)


def first_tables(s):
    cosine, sine = waves(kept(s.jx, s.gx), s.gx)
    lxk = s.lx // X_CHUNKS
    c5 = cosine.reshape(s.chan, s.jxl, s.owners, X_CHUNKS, lxk)
    s5 = sine.reshape(s.chan, s.jxl, s.owners, X_CHUNKS, lxk)
    forward = np.zeros((s.chan, 2, s.jxl, X_CHUNKS, s.owners, 2, lxk))
    inverse = np.zeros((X_CHUNKS, s.owners, 2, lxk, s.chan, 2, s.jxl))
    for out, inp, sign_f, wave in ((0, 0, 1, c5), (0, 1, 1, s5), (1, 0, -1, s5), (1, 1, 1, c5)):
        forward[:, out, :, :, :, inp] = sign_f * wave.transpose(0, 1, 3, 2, 4)
        inverse[:, :, inp, :, :, out] = sign_f * wave.transpose(3, 2, 4, 0, 1)
    rows = s.chan * 2 * s.jxl
    return forward.reshape(rows, -1), inverse.reshape(-1, rows)


def terms(value):
    high = value.astype(bf16)
    return high, (value - high.astype(f32)).astype(bf16)


def dot(a, b):
    return jnp.dot(a, b, preferred_element_type=f32)


def square_dot(table, value):
    high, low = terms(value)
    both = dot(table, jnp.concatenate([high, low], 0))
    half = both.shape[0] // 2
    return both[:half] + both[half:]


def gelu_parts(v):
    normal_cdf = 0.5 * (1.0 + lax.erf(v * (1.0 / math.sqrt(2.0))))
    slope = normal_cdf + v * jnp.exp(-0.5 * v * v) * (1.0 / math.sqrt(2.0 * math.pi))
    return normal_cdf, slope


def forward_second(s, x, pair, tile, table_ref, wide_high, wide_low):
    out = square_dot(table_ref[...], tile)
    rows = pl.ds(pl.multiple_of(x * s.jy, s.jy), s.jy)
    for c in range(2):
        for part in range(2):
            high, low = terms(out[part * s.jy:(part + 1) * s.jy, c * s.gz:(c + 1) * s.gz])
            at = ((pair * 2 + c) * 2 + part) * s.gz
            wide_high[rows, at:at + s.gz] = high
            wide_low[rows, at:at + s.gz] = low


def forward_third(s, lxk, wide_high, wide_low, high_ref, low_ref, out_ref):
    high = wide_high[...]
    out = dot(high, high_ref[...]) + dot(wide_low[...], high_ref[...]) + dot(high, low_ref[...])
    for x in range(lxk):
        for part in range(2):
            for p in range(s.planes):
                start = x * s.jy + p * s.jl
                out_ref[p, 0, pl.ds(part * lxk + x, s.jl, stride=2 * lxk), :] = out[
                    start:start + s.jl, part * LANES:(part + 1) * LANES
                ]


def gather_modes(s, lxk, in_ref, sum_high, sum_low):
    for x in range(lxk):
        for part in range(2):
            for p in range(s.planes):
                piece = in_ref[p, 0, pl.ds(part * lxk + x, s.jl, stride=2 * lxk), :]
                high, low = terms(piece)
                start = x * s.jy + p * s.jl
                sum_high[start:start + s.jl, part * LANES:(part + 1) * LANES] = high
                sum_low[start:start + s.jl, part * LANES:(part + 1) * LANES] = low


def inverse_third(s, sum_high, sum_low, high_ref, low_ref, depth):
    high = sum_high[...]
    low = sum_low[...]
    for c in range(s.gw):
        depth[c] = dot(high, high_ref[c]) + dot(low, high_ref[c]) + dot(high, low_ref[c])


def inverse_second(s, x, pair, table_ref, depth):
    rows = pl.ds(pl.multiple_of(x * s.jy, s.jy), s.jy)
    sides = []
    for c in range(2):
        both = depth[pair * 2 + c, rows, :]
        sides.append(jnp.concatenate([both[:, :s.gz], both[:, s.gz:]], 0))
    return square_dot(table_ref[...], jnp.concatenate(sides, 1))


def analysis_kernel(s, lxk, field_ref, second_ref, high_ref, low_ref, out_ref, wide_high, wide_low):
    def one(x, carry):
        for pair in range(s.gw // 2):
            tile = jnp.concatenate([field_ref[0, pair * 2, x], field_ref[0, pair * 2 + 1, x]], 1)
            forward_second(s, x, pair, tile, second_ref, wide_high, wide_low)
        return carry

    lax.fori_loop(0, lxk, one, 0)
    forward_third(s, lxk, wide_high, wide_low, high_ref, low_ref, out_ref)


def middle_kernel(
    s, lxk, in_ref, point_ref, cot_ref, inv_high, inv_low, inv_second, second_ref, high_ref, low_ref,
    output_ref, grad_ref, out_ref, sum_high, sum_low, depth, wide_high, wide_low,
):
    gather_modes(s, lxk, in_ref, sum_high, sum_low)
    inverse_third(s, sum_high, sum_low, inv_high, inv_low, depth)

    def one(x, carry):
        for pair in range(s.gw // 2):
            plane = inverse_second(s, x, pair, inv_second, depth)
            grads = []
            for c in range(2):
                v = plane[:, c * s.gz:(c + 1) * s.gz] + point_ref[0, pair * 2 + c, x]
                normal_cdf, slope = gelu_parts(v)
                output_ref[0, pair * 2 + c, x] = v * normal_cdf
                grad = cot_ref[0, pair * 2 + c, x] * slope
                grad_ref[0, pair * 2 + c, x] = grad
                grads.append(grad)
            forward_second(s, x, pair, jnp.concatenate(grads, 1), second_ref, wide_high, wide_low)
        return carry

    lax.fori_loop(0, lxk, one, 0)
    forward_third(s, lxk, wide_high, wide_low, high_ref, low_ref, out_ref)


def final_kernel(s, lxk, in_ref, local_ref, inv_high, inv_low, inv_second, out_ref, sum_high, sum_low, depth):
    gather_modes(s, lxk, in_ref, sum_high, sum_low)
    inverse_third(s, sum_high, sum_low, inv_high, inv_low, depth)

    def one(x, carry):
        for pair in range(s.gw // 2):
            plane = inverse_second(s, x, pair, inv_second, depth)
            for c in range(2):
                out_ref[0, pair * 2 + c, x] = (
                    plane[:, c * s.gz:(c + 1) * s.gz] + local_ref[0, pair * 2 + c, x]
                )
        return carry

    lax.fori_loop(0, lxk, one, 0)


def whole(array):
    rank = len(array.shape)
    return pl.BlockSpec(array.shape, lambda *_: (0,) * rank, pipeline_mode=pl.Buffered(1))


def cost(flops, *arrays):
    count = sum(int(np.prod(a.shape)) * a.dtype.itemsize for a in arrays)
    return pl.CostEstimate(flops=int(flops), bytes_accessed=count, transcendentals=0)


def grid_spec(s, lxk, chunk):
    return pl.BlockSpec((1, s.gw, lxk, s.gy, s.gz), lambda g: (0, g, chunk, 0, 0))


def mode_spec(s, lxk):
    return pl.BlockSpec((s.planes, 1, s.jl * 2 * lxk, LANES), lambda g: (0, g, 0, 0))


def mode_shape(s, lxk):
    return jax.ShapeDtypeStruct((s.planes, s.chan, s.jl * 2 * lxk, LANES), f32)


def wide_scratch(s, lxk):
    return [pltpu.VMEM((lxk * s.jy, s.gw * 2 * s.gz), bf16)] * 2


def sum_scratch(s, lxk):
    return [
        pltpu.VMEM((lxk * s.jy, 2 * LANES), bf16),
        pltpu.VMEM((lxk * s.jy, 2 * LANES), bf16),
        pltpu.VMEM((s.gw, lxk * s.jy, 2 * s.gz), f32),
    ]


def analysis(s, field, chunk, second, third):
    lxk = s.lx // X_CHUNKS
    out = mode_shape(s, lxk)
    tables = (second[0], third[0], third[1])
    return pl.pallas_call(
        functools.partial(analysis_kernel, s, lxk),
        grid=(s.chan,),
        in_specs=[grid_spec(s, lxk, chunk)] + [whole(t) for t in tables],
        out_specs=mode_spec(s, lxk),
        out_shape=out,
        scratch_shapes=wide_scratch(s, lxk),
        cost_estimate=cost(6e9 / X_CHUNKS, field, out),
        name="analysis",
    )(field, *tables)


def middle(s, modes, point, cotangent, chunk, second, third, output, grad):
    lxk = s.lx // X_CHUNKS
    out = mode_shape(s, lxk)
    tables = (third[2], third[3], second[1], second[0], third[0], third[1])
    spec = grid_spec(s, lxk, chunk)
    aliased = [] if output is None else [output, grad]
    count = 3 + len(tables)

    def body(*refs):
        middle_kernel(s, lxk, *refs[:count], *refs[count + len(aliased):])

    return pl.pallas_call(
        body,
        grid=(s.chan,),
        in_specs=[mode_spec(s, lxk), spec, spec]
        + [whole(t) for t in tables]
        + [pl.BlockSpec(memory_space=pl.ANY)] * len(aliased),
        out_specs=[spec, spec, mode_spec(s, lxk)],
        out_shape=[jax.ShapeDtypeStruct(point.shape, f32)] * 2 + [out],
        scratch_shapes=sum_scratch(s, lxk) + wide_scratch(s, lxk),
        input_output_aliases={count + i: i for i in range(len(aliased))},
        cost_estimate=cost(1.2e10 / X_CHUNKS, modes, point, cotangent, point, point),
        name="middle",
    )(modes, point, cotangent, *tables, *aliased)


def final(s, modes, local_grad, chunk, second, third, grad):
    lxk = s.lx // X_CHUNKS
    tables = (third[2], third[3], second[1])
    spec = grid_spec(s, lxk, chunk)
    aliased = [] if grad is None else [grad]
    count = 2 + len(tables)

    def body(*refs):
        final_kernel(s, lxk, *refs[:count], *refs[count + len(aliased):])

    return pl.pallas_call(
        body,
        grid=(s.chan,),
        in_specs=[mode_spec(s, lxk), spec]
        + [whole(t) for t in tables]
        + [pl.BlockSpec(memory_space=pl.ANY)] * len(aliased),
        out_specs=spec,
        out_shape=jax.ShapeDtypeStruct(local_grad.shape, f32),
        scratch_shapes=sum_scratch(s, lxk),
        input_output_aliases={count + i: i for i in range(len(aliased))},
        cost_estimate=cost(6e9 / X_CHUNKS, modes, local_grad, local_grad),
        name="final",
    )(modes, local_grad, *tables, *aliased)


def pointwise_kernel(channels, values_ref, weight_ref, bias_ref, out_ref):
    def rows(step, carry):
        at = pl.ds(pl.multiple_of(step * 32, 32), 32)
        sources = [values_ref[0, i, 0, at, :] for i in range(channels)]
        for o in range(channels):
            total = sources[0] * weight_ref[0, o] + bias_ref[o]
            for i in range(1, channels):
                total = total + sources[i] * weight_ref[i, o]
            out_ref[0, o, 0, at, :] = total
        return carry

    lax.fori_loop(0, values_ref.shape[3] // 32, rows, 0)


def pointwise(values, weight, bias):
    _, channels, lx, gy, gz = values.shape
    spec = pl.BlockSpec((1, channels, 1, gy, gz), lambda x: (0, 0, x, 0, 0))
    return pl.pallas_call(
        functools.partial(pointwise_kernel, channels),
        grid=(lx,),
        in_specs=[spec, pl.BlockSpec(memory_space=pltpu.SMEM), pl.BlockSpec(memory_space=pltpu.SMEM)],
        out_specs=spec,
        out_shape=jax.ShapeDtypeStruct(values.shape, f32),
        cost_estimate=cost(1e10, values, values),
        name="pointwise",
    )(values, weight, bias)


def first_kernel(rows, chunks, *refs):
    ins, (stacked_ref, out_ref) = refs[:chunks], refs[chunks:]
    sides = []
    per = ins[0].shape[1] // 2
    for j in range(2):
        parts = [r[o, j * per:(j + 1) * per, :] for r in ins for o in range(r.shape[0])]
        sides.append(jnp.concatenate(parts, 0))
    high, low = terms(jnp.concatenate(sides, 1))
    both = dot(stacked_ref[...], high)
    out = both[:rows] + both[rows:] + dot(stacked_ref[:rows, :], low)
    step = out_ref.shape[1] // 2
    for c in range(out_ref.shape[0]):
        for j in range(2):
            out_ref[c, j * step:(j + 1) * step, :] = out[
                c * step:(c + 1) * step, j * LANES:(j + 1) * LANES
            ]


def first_pass(s, chunks, table, mode_chunk):
    lxk = s.lx // X_CHUNKS
    rows = table.shape[0]
    stacked = np.concatenate(two_terms(table), 0)
    pairs = s.jl // MODE_CHUNKS // 2
    out = jax.ShapeDtypeStruct((s.chan, pairs * 2 * 2 * s.jxl, LANES), f32)
    offset = mode_chunk * pairs
    return pl.pallas_call(
        functools.partial(first_kernel, rows, len(chunks)),
        grid=(pairs,),
        in_specs=[pl.BlockSpec((s.owners, 4 * lxk, LANES), lambda j: (0, j + offset, 0))] * len(chunks)
        + [whole(stacked)],
        out_specs=pl.BlockSpec((s.chan, 4 * s.jxl, LANES), lambda j: (0, j, 0)),
        out_shape=out,
        cost_estimate=cost(1e9 / MODE_CHUNKS, out, out, out),
        name="first_forward",
    )(*chunks, stacked)


def back_kernel(chunks, in_ref, *refs):
    tables, outs = refs[:chunks], refs[chunks:]
    step = in_ref.shape[1] // 2
    sides = []
    for j in range(2):
        parts = [in_ref[c, j * step:(j + 1) * step, :] for c in range(in_ref.shape[0])]
        sides.append(jnp.concatenate(parts, 0))
    value = jnp.concatenate(sides, 1)
    for table_ref, out_ref in zip(tables, outs):
        out = square_dot(table_ref[...], value)
        per = out_ref.shape[1] // 2
        for o in range(out_ref.shape[0]):
            for j in range(2):
                out_ref[o, j * per:(j + 1) * per, :] = out[
                    o * per:(o + 1) * per, j * LANES:(j + 1) * LANES
                ]


def first_inverse(s, modes, table):
    lxk = s.lx // X_CHUNKS
    rows = table.shape[0] // X_CHUNKS
    squares = [stacked_square(table[k * rows:(k + 1) * rows]) for k in range(X_CHUNKS)]
    pairs = s.jl // 2
    out = jax.ShapeDtypeStruct((s.owners, s.jl * 2 * lxk, LANES), f32)
    return pl.pallas_call(
        functools.partial(back_kernel, X_CHUNKS),
        grid=(pairs,),
        in_specs=[pl.BlockSpec((s.chan, 4 * s.jxl, LANES), lambda j: (0, j, 0))]
        + [whole(t) for t in squares],
        out_specs=[pl.BlockSpec((s.owners, 4 * lxk, LANES), lambda j: (0, j, 0))] * X_CHUNKS,
        out_shape=[out] * X_CHUNKS,
        cost_estimate=cost(1e9, out, out, out),
        name="first_inverse",
    )(modes, *squares)


def swap_groups(pieces, width):
    count = len(pieces)
    lane = lax.broadcasted_iota(jnp.int32, pieces[0].shape, 1)
    step = count // 2
    pieces = list(pieces)
    while step:
        upper = (lane // (width * step)) % 2 == 1
        for a in range(count):
            if a & step:
                continue
            low, high = pieces[a], pieces[a + step]
            pieces[a] = jnp.where(upper, pltpu.roll(high, width * step, 1), low)
            pieces[a + step] = jnp.where(upper, high, pltpu.roll(low, LANES - width * step, 1))
        step //= 2
    return pieces


def spread_modes(s, count, in_ref, out_ref, factor=None):
    stride = 2 * s.jxl
    for g in range(s.chan):
        for part in range(2):
            for a in range(s.jxl // s.gw):
                pieces = [
                    in_ref[g, pl.ds(part * s.jxl + a * s.gw + b, count, stride=stride), :]
                    for b in range(s.gw)
                ]
                for c, piece in enumerate(swap_groups(pieces, s.modes)):
                    if factor is not None:
                        piece = piece * factor
                    out_ref[part, g * s.gw + c, :, a * LANES:(a + 1) * LANES] = piece


def depth_factor(s, shape):
    lane = lax.broadcasted_iota(jnp.int32, shape, 1)
    return jnp.where(lane % s.modes == 0, s.scale, 2.0 * s.scale).astype(f32)


def mix_kernel(s, count, in_ref, weight_ref, out_ref, kept_ref):
    @pl.when(pl.program_id(0) == 0)
    def _():
        spread_modes(s, count, in_ref, kept_ref)

    factor = depth_factor(s, (count, LANES))
    pieces = s.flat // LANES
    block = [[[None] * pieces for _ in range(s.gw)] for _ in range(2)]
    for a in range(pieces):
        at = slice(a * LANES, (a + 1) * LANES)
        reals = [None] * s.gw
        imags = [None] * s.gw
        for i in range(s.ch):
            real = kept_ref[0, i, :, at]
            imag = kept_ref[1, i, :, at]
            for o in range(s.gw):
                w_real = weight_ref[0, i, o, :, at]
                w_imag = weight_ref[1, i, o, :, at]
                new_real = real * w_real - imag * w_imag
                new_imag = real * w_imag + imag * w_real
                reals[o] = new_real if i == 0 else reals[o] + new_real
                imags[o] = new_imag if i == 0 else imags[o] + new_imag
        for o in range(s.gw):
            block[0][o][a] = reals[o] * factor
            block[1][o][a] = imags[o] * factor
    store_block(s, count, block, out_ref)


def store_block(s, count, block, out_ref):
    stride = 2 * s.jxl
    for part in range(2):
        for a in range(s.flat // LANES):
            for b, piece in enumerate(swap_groups([block[part][c][a] for c in range(s.gw)], s.modes)):
                out_ref[0, pl.ds(part * s.jxl + a * s.gw + b, count, stride=stride), :] = piece


def mix(s, modes, spec_weight, mode_chunk):
    count = s.jl // MODE_CHUNKS
    kept_shape = jax.ShapeDtypeStruct((2, s.ch, count, s.flat), f32)
    return pl.pallas_call(
        functools.partial(mix_kernel, s, count),
        grid=(s.chan,),
        in_specs=[
            whole(modes),
            pl.BlockSpec((2, s.ch, s.gw, count, s.flat), lambda g: (0, 0, g, mode_chunk, 0)),
        ],
        out_specs=[
            pl.BlockSpec((1, count * 2 * s.jxl, LANES), lambda g: (g, 0, 0)),
            whole(kept_shape),
        ],
        out_shape=[jax.ShapeDtypeStruct(modes.shape, f32), kept_shape],
        cost_estimate=cost(1e8, modes, modes, spec_weight),
        name="mix",
    )(modes, spec_weight)


def unmix_kernel(s, count, in_ref, weight_ref, out_ref, kept_ref):
    factor = depth_factor(s, (count, LANES))

    @pl.when(pl.program_id(0) == 0)
    def _():
        spread_modes(s, count, in_ref, kept_ref, factor)

    pieces = s.flat // LANES
    block = [[[None] * pieces for _ in range(s.gw)] for _ in range(2)]
    for a in range(pieces):
        at = slice(a * LANES, (a + 1) * LANES)
        reals = [None] * s.gw
        imags = [None] * s.gw
        for o in range(s.ch):
            real = kept_ref[0, o, :, at]
            imag = kept_ref[1, o, :, at]
            for i in range(s.gw):
                w_real = weight_ref[0, i, o, :, at]
                w_imag = weight_ref[1, i, o, :, at]
                new_real = real * w_real + imag * w_imag
                new_imag = imag * w_real - real * w_imag
                reals[i] = new_real if o == 0 else reals[i] + new_real
                imags[i] = new_imag if o == 0 else imags[i] + new_imag
        for i in range(s.gw):
            block[0][i][a] = reals[i]
            block[1][i][a] = imags[i]
    store_block(s, count, block, out_ref)


def unmix(s, modes, spec_weight, mode_chunk):
    count = s.jl // MODE_CHUNKS
    kept_shape = jax.ShapeDtypeStruct((2, s.ch, count, s.flat), f32)
    return pl.pallas_call(
        functools.partial(unmix_kernel, s, count),
        grid=(s.chan,),
        in_specs=[
            whole(modes),
            pl.BlockSpec((2, s.gw, s.ch, count, s.flat), lambda g: (0, g, 0, mode_chunk, 0)),
        ],
        out_specs=[
            pl.BlockSpec((1, count * 2 * s.jxl, LANES), lambda g: (g, 0, 0)),
            whole(kept_shape),
        ],
        out_shape=[jax.ShapeDtypeStruct(modes.shape, f32), kept_shape],
        cost_estimate=cost(1e8, modes, modes, spec_weight),
        name="unmix",
    )(modes, spec_weight)


def weight_kernel(s, width, spec_ref, grad_ref, out_ref):
    for i in range(width):
        for a in range(s.flat // LANES):
            at = slice(a * LANES, (a + 1) * LANES)
            real = spec_ref[0, i, :, at]
            imag = spec_ref[1, i, :, at]
            for o in range(s.ch):
                g_real = grad_ref[0, o, :, at]
                g_imag = grad_ref[1, o, :, at]
                out_ref[0, i, o, :, at] = real * g_real + imag * g_imag
                out_ref[1, i, o, :, at] = real * g_imag - imag * g_real


def weight_grads(s, spec, grad, mode_chunk, total):
    count = s.jl // MODE_CHUNKS
    width = 2
    aliased = [] if total is None else [total]

    def body(spec_ref, grad_ref, *refs):
        weight_kernel(s, width, spec_ref, grad_ref, refs[-1])

    shape = jax.ShapeDtypeStruct((2, s.ch, s.ch, s.jl, s.flat), f32)
    return pl.pallas_call(
        body,
        grid=(s.ch // width,),
        in_specs=[pl.BlockSpec((2, width, count, s.flat), lambda i: (0, i, 0, 0)), whole(grad)]
        + [pl.BlockSpec(memory_space=pl.ANY)] * len(aliased),
        out_specs=pl.BlockSpec((2, width, s.ch, count, s.flat), lambda i: (0, i, 0, mode_chunk, 0)),
        out_shape=shape,
        input_output_aliases={2 + i: i for i in range(len(aliased))},
        cost_estimate=cost(1e8, shape),
        name="weight_grads",
    )(spec, grad, *aliased)


def over_owners(s, value):
    flat = value.reshape((s.owners,) + value.shape[-2:])
    return lax.all_to_all(flat, ("planes", "chan"), 0, 0, tiled=True)


def over_chan(value):
    return lax.all_to_all(value, "chan", 0, 0, tiled=True)


def joined(parts):
    return parts[0] if len(parts) == 1 else jnp.concatenate(parts, 1)


def fast_local(s, field, cotangent, spec_weight, point_weight, bias):
    second = second_tables(s)
    third = third_tables(s)
    forward, inverse = first_tables(s)
    x_chunks = range(X_CHUNKS)
    mode_chunks = range(MODE_CHUNKS)
    by_planes = (s.planes, s.chan)

    arrived = [over_owners(s, analysis(s, field, k, second, third)) for k in x_chunks]
    point = pointwise(field, point_weight, bias)
    owned = [over_chan(first_pass(s, arrived, forward, m)) for m in mode_chunks]
    mixed = [mix(s, owned[m], spec_weight, m) for m in mode_chunks]
    returned = joined([over_chan(v[0]) for v in mixed])
    back = [over_owners(s, v) for v in first_inverse(s, returned, inverse)]
    output = grad = None
    arrived = []
    for k in x_chunks:
        modes = back[k].reshape(by_planes + back[k].shape[1:])
        output, grad, sent = middle(s, modes, point, cotangent, k, second, third, output, grad)
        arrived.append(over_owners(s, sent))
    local_grad = pointwise(grad, point_weight.T, jnp.zeros_like(bias))
    owned = [over_chan(first_pass(s, arrived, forward, m)) for m in mode_chunks]
    unmixed = [unmix(s, owned[m], spec_weight, m) for m in mode_chunks]
    returned = joined([over_chan(v[0]) for v in unmixed])
    weight_grad = None
    for m in mode_chunks:
        weight_grad = weight_grads(s, mixed[m][1], unmixed[m][1], m, weight_grad)
    back = [over_owners(s, v) for v in first_inverse(s, returned, inverse)]
    field_grad = None
    for k in x_chunks:
        modes = back[k].reshape(by_planes + back[k].shape[1:])
        field_grad = final(s, modes, local_grad, k, second, third, field_grad)
    return output, field_grad, weight_grad


def local(field, cotangent, spec_weight, point_weight, bias):
    s = Sizes(field, spec_weight)
    if s.fits():
        return fast_local(s, field, cotangent, spec_weight, point_weight, bias)
    return plain_local(s, field, cotangent, spec_weight, point_weight, bias)


def solution(mesh):
    in_specs = (
        P("groups", None, ("planes", "chan"), None, None),
        P("groups", None, ("planes", "chan"), None, None),
        P(None, None, None, "planes", "chan"),
        P(),
        P(),
    )
    out_specs = (
        P("groups", None, ("planes", "chan"), None, None),
        P("groups", None, ("planes", "chan"), None, None),
        P("groups", None, None, "planes", "chan"),
    )
    return jax.shard_map(local, mesh=mesh, in_specs=in_specs, out_specs=out_specs, check_vma=False)
```

```python
import functools
import math

import numpy as np

import jax
import jax.numpy as jnp
from jax import lax
from jax.experimental import pallas as pl
from jax.experimental.pallas import tpu as pltpu
from jax.sharding import PartitionSpec as P


exact_mode = lax.Precision.HIGHEST


def retained(s, length):
    indices = jnp.arange(2 * s.modes)
    return jnp.where(indices < s.modes, indices, length - 2 * s.modes + indices)


def phase_table(positions, freqs, length):
    turn_count = positions[:, None] * freqs[None, :] % length
    angles = turn_count.astype(jnp.float32) * (2.0 * math.pi / length)
    return (jnp.cos(angles), jnp.sin(angles))


def plain_analysis(s, field):
    batch_size, channels, local_planes, second_length, third_length = field.shape
    plane_count = lax.axis_size("planes")
    channel_groups = lax.axis_size("chan")
    group_width = channels // channel_groups
    local_modes = 2 * s.modes // plane_count
    first_length = local_planes * plane_count * channel_groups
    cosine, sine_part = phase_table(
        jnp.arange(second_length), retained(s, second_length), second_length
    )
    second_table = jnp.stack([cosine, -sine_part], 1).reshape(
        second_length, 2, plane_count, local_modes
    )
    cosine, sine_part = phase_table(jnp.arange(third_length), jnp.arange(s.modes), third_length)
    third_table = jnp.stack(
        [jnp.stack([cosine, -sine_part], 1), jnp.stack([sine_part, cosine], 1)], 0
    )
    grouped = field.reshape(
        batch_size, channel_groups, group_width, local_planes, second_length, third_length
    )
    second_pass = jnp.einsum("bcdxyz,yspk->bcdxspkz", grouped, second_table, precision=exact_mode)
    spectra = jnp.einsum("bcdxspkz,sztm->bpckxdtm", second_pass, third_table, precision=exact_mode)
    spectra = spectra.reshape(
        batch_size, plane_count * channel_groups, local_modes, local_planes, group_width * 2 * s.modes
    )
    arrived = lax.all_to_all(spectra, ("planes", "chan"), split_axis=1, concat_axis=3, tiled=True)
    positions = jnp.arange(first_length)
    arrived = arrived.reshape(batch_size, local_modes, first_length, group_width, 2, s.modes)
    cosine, sine_part = phase_table(positions, retained(s, first_length), first_length)
    first_table = jnp.stack(
        [jnp.stack([cosine, -sine_part], 1), jnp.stack([sine_part, cosine], 1)], 1
    )
    first_pass = jnp.einsum("bkxdsm,xstf->bkdtfm", arrived, first_table, precision=exact_mode)
    first_pass = first_pass.reshape(batch_size, local_modes, group_width, 2, 2 * s.modes * s.modes)
    return lax.all_to_all(first_pass, "chan", split_axis=4, concat_axis=2, tiled=True)


def plain_synthesis(s, spectrum):
    batch_size, local_modes, channels = (spectrum.shape[0], spectrum.shape[1], spectrum.shape[2])
    plane_count = lax.axis_size("planes")
    channel_groups = lax.axis_size("chan")
    group_width = channels // channel_groups
    local_planes = s.gx // (plane_count * channel_groups)
    gathered = lax.all_to_all(spectrum, "chan", split_axis=2, concat_axis=4, tiled=True)
    gathered = gathered.reshape(batch_size, local_modes, group_width, 2, 2 * s.modes, s.modes)
    cosine, sine_part = phase_table(jnp.arange(s.gx), retained(s, s.gx), s.gx)
    cosine_t = cosine.T
    sine_t = sine_part.T
    first_inverse = jnp.stack(
        [jnp.stack([cosine_t, sine_t], -1), jnp.stack([-sine_t, cosine_t], -1)], 0
    )
    first_pass = jnp.einsum("bkdsfm,sfxt->bkxdtm", gathered, first_inverse, precision=exact_mode)
    first_pass = first_pass.reshape(batch_size, local_modes, s.gx, group_width * 2 * s.modes)
    returned = lax.all_to_all(
        first_pass[:, None], ("planes", "chan"), split_axis=3, concat_axis=1, tiled=True
    )
    returned = returned.reshape(
        batch_size, plane_count, channel_groups, local_modes, local_planes, group_width, 2, s.modes
    )
    source_form = "bpckxdtm"
    cosine, sine_part = phase_table(jnp.arange(s.gz), jnp.arange(s.modes), s.gz)
    cosine_t = cosine.T
    sine_t = sine_part.T
    third_inverse = jnp.stack(
        [jnp.stack([cosine_t, sine_t], 1), jnp.stack([-sine_t, cosine_t], 1)], 0
    )
    depth_pass = jnp.einsum(
        source_form + ",tmuz->bcdxpkuz", returned, third_inverse, precision=exact_mode
    )
    cosine, sine_part = phase_table(jnp.arange(s.gy), retained(s, s.gy), s.gy)
    second_inverse = jnp.stack([cosine.T, -sine_part.T], 0).reshape(2, plane_count, local_modes, s.gy)
    physical = jnp.einsum("bcdxpkuz,upky->bcdxyz", depth_pass, second_inverse, precision=exact_mode)
    return physical.reshape(batch_size, channels, local_planes, s.gy, s.gz)


def mode_weighting(s, mode_count):
    depth_mode = jnp.arange(mode_count) % s.modes
    return jnp.where(depth_mode == 0, 1.0, 2.0).astype(jnp.float32) / float(s.gx * s.gy * s.gz)


def contract(operand, weights):
    return jnp.einsum("bkin,iokn->bkon", operand, weights, precision=exact_mode)


def adjoint(operand, weights):
    return jnp.einsum("bkon,iokn->bkin", operand, weights, precision=exact_mode)


def outer_sum(first_operand, second_operand):
    return jnp.einsum("bkin,bkon->iokn", first_operand, second_operand, precision=exact_mode)


def plain_local(s, field, cotangent, spec_weight, point_weight, bias):
    spectrum = plain_analysis(s, field)
    weight_re = spec_weight[0]
    weight_im = spec_weight[1]
    spec_re = spectrum[:, :, :, 0]
    spec_im = spectrum[:, :, :, 1]
    weighting = mode_weighting(s, spectrum.shape[-1])
    mixed_re = (contract(spec_re, weight_re) - contract(spec_im, weight_im)) * weighting
    mixed_im = (contract(spec_re, weight_im) + contract(spec_im, weight_re)) * weighting
    mixed_modes = jnp.stack([mixed_re, mixed_im], 3)
    spectral = plain_synthesis(s, mixed_modes)
    pointwise = jnp.einsum("bixyz,io->boxyz", field, point_weight, precision=exact_mode)
    preactivation = spectral + pointwise + bias[None, :, None, None, None]
    normal_cdf = 0.5 * (1.0 + lax.erf(preactivation * (1.0 / math.sqrt(2.0))))
    output = preactivation * normal_cdf
    derivative = normal_cdf + preactivation * jnp.exp(-0.5 * preactivation * preactivation) * (
        1.0 / math.sqrt(2.0 * math.pi)
    )
    pre_grad = cotangent * derivative
    raw_grad = plain_analysis(s, pre_grad)
    grad_re = raw_grad[:, :, :, 0] * weighting
    grad_im = raw_grad[:, :, :, 1] * weighting
    spectrum_grad = jnp.stack(
        [
            adjoint(grad_re, weight_re) + adjoint(grad_im, weight_im),
            adjoint(grad_im, weight_re) - adjoint(grad_re, weight_im),
        ],
        3,
    )
    weight_grad = jnp.stack(
        [
            outer_sum(spec_re, grad_re) + outer_sum(spec_im, grad_im),
            outer_sum(spec_re, grad_im) - outer_sum(spec_im, grad_re),
        ],
        0,
    )
    local_grad = jnp.einsum("boxyz,io->bixyz", pre_grad, point_weight, precision=exact_mode)
    field_grad = local_grad + plain_synthesis(s, spectrum_grad)
    return (output, field_grad, weight_grad)


LANES = 128
BLOCK = 4
MODE_CHUNKS = 2
f32 = jnp.float32
bf16 = jnp.bfloat16


class Sizes:
    def __init__(self, field, spec_weight):
        self.planes = lax.axis_size("planes")
        self.chan = lax.axis_size("chan")
        self.owners = self.planes * self.chan
        _, self.ch, self.lx, self.gy, self.gz = field.shape
        self.gx = self.lx * self.owners
        _, _, _, self.jl, local_flat = spec_weight.shape
        self.jy = self.jl * self.planes
        self.flat = local_flat
        self.modes = self.jy // 2
        self.jxl = local_flat // self.modes
        self.jx = self.jxl * self.chan
        self.gw = self.ch // self.chan
        self.scale = 1.0 / float(self.gx * self.gy * self.gz)

    def fits(self):
        return (
            self.gw == 4
            and self.gw * self.modes == LANES
            and self.gz == LANES
            and self.gy == LANES
            and self.jy * 2 == LANES
            and self.jx * 2 == LANES
            and self.flat % LANES == 0
            and self.ch * 16 == 2 * LANES
            and self.jl % (8 * MODE_CHUNKS) == 0
            and self.lx % (2 * BLOCK) == 0
            and self.gx == LANES
            and self.chan & (self.chan - 1) == 0
            and self.planes & (self.planes - 1) == 0
        )


def kept(count, length):
    index = np.arange(count)
    return np.where(index < count // 2, index, length - count + index)


def waves(freqs, length):
    turns = (freqs[:, None] * np.arange(length)[None, :]) % length
    angles = turns * (2.0 * math.pi / length)
    return np.cos(angles), np.sin(angles)


def two_terms(table):
    table = np.asarray(table, np.float32)
    high = table.astype(jnp.bfloat16)
    low = (table - high.astype(np.float32)).astype(jnp.bfloat16)
    return high, low


def stacked_square(table):
    high, low = two_terms(table)
    return np.concatenate([np.concatenate([high, high], 1), np.concatenate([low, low], 1)], 0)


def second_tables(s):
    cosine, sine = waves(kept(s.jy, s.gy), s.gy)
    forward = np.concatenate([cosine, sine], 0)
    inverse = np.concatenate(
        [np.concatenate([cosine.T, -sine.T], 1), np.concatenate([sine.T, cosine.T], 1)], 0
    )
    return stacked_square(forward), stacked_square(inverse)


def third_tables(s):
    cosine, sine = waves(np.arange(s.modes), s.gz)
    table = np.zeros((2, s.gz, 2, 2, s.modes))
    for c in range(2):
        table[c, :, 0, c] = cosine.T
        table[c, :, 1, c] = -sine.T
    table = table.reshape(2 * s.gz, LANES)
    forward = np.concatenate(two_terms(table), 1)
    high, low = two_terms(table.T)
    wide = np.concatenate([high, low], 1)
    return forward, np.concatenate([wide, wide], 0)


def first_tables(s):
    cosine, sine = waves(kept(s.jx, s.gx), s.gx)
    c4 = cosine.reshape(s.chan, s.jxl, s.owners, s.lx)
    s4 = sine.reshape(s.chan, s.jxl, s.owners, s.lx)
    forward = np.zeros((s.chan, 2, s.jxl, s.owners, 2, s.lx))
    inverse = np.zeros((s.owners, 2, s.lx, s.chan, 2, s.jxl))
    for out, inp, sign, wave in ((0, 0, 1, c4), (0, 1, 1, s4), (1, 0, -1, s4), (1, 1, 1, c4)):
        forward[:, out, :, :, inp] = sign * wave
        inverse[:, inp, :, :, out] = sign * wave.transpose(2, 3, 0, 1)
    rows = s.chan * 2 * s.jxl
    return forward.reshape(rows, -1), inverse.reshape(-1, rows)


def terms(value):
    high = value.astype(bf16)
    return high, (value - high.astype(f32)).astype(bf16)


def dot(a, b):
    return jnp.dot(a, b, preferred_element_type=f32)


def square_dot(table, value):
    high, low = terms(value)
    both = dot(table, jnp.concatenate([high, low], 0))
    half = both.shape[0] // 2
    return both[:half] + both[half:]


def gelu_parts(v):
    normal_cdf = 0.5 * (1.0 + lax.erf(v * (1.0 / math.sqrt(2.0))))
    slope = normal_cdf + v * jnp.exp(-0.5 * v * v) * (1.0 / math.sqrt(2.0 * math.pi))
    return normal_cdf, slope


def half_lanes(shape):
    return lax.broadcasted_iota(jnp.int32, shape, 1) < LANES // 2


def place_terms(s, row, value, split):
    half = split.shape[0] // 2
    high, low = terms(value)
    split[pl.ds(pl.multiple_of(row * s.gy, s.gy), s.gy), :] = high
    split[pl.ds(pl.multiple_of(half + row * s.gy, s.gy), s.gy), :] = low


def forward_planes(s, split, third_ref, second_ref, held):
    half = split.shape[0] // 2
    both = dot(split[...], third_ref[...])
    deep = both[:half, :LANES] + both[:half, LANES:] + both[half:, :LANES]
    first = half_lanes((s.jy, LANES))
    for x in range(BLOCK):
        side = [deep[(2 * x + q) * s.gy:(2 * x + q + 1) * s.gy] for q in range(2)]
        out = square_dot(second_ref[...], jnp.concatenate(side, 1))
        pairs = []
        for k in range(2):
            turned = pltpu.roll(out[s.jy:, k * LANES:(k + 1) * LANES], LANES // 2, 1)
            pairs.append(out[:s.jy, k * LANES:(k + 1) * LANES] + jnp.where(first, turned, -turned))
        rows = slice(x * s.jy, (x + 1) * s.jy)
        held[rows, :LANES] = jnp.where(first, pairs[0], pltpu.roll(pairs[1], LANES // 2, 1))
        held[rows, LANES:] = jnp.where(first, pltpu.roll(pairs[0], LANES // 2, 1), pairs[1])


def scatter_modes(s, outs, held):
    me = lax.axis_index("planes")
    first = pl.program_id(1) * BLOCK
    for k, group in enumerate(outs):

        @pl.when(pl.program_id(0) == k)
        def _(group=group):
            for d, out_ref in enumerate(group):
                for x in range(BLOCK):
                    at = pl.ds(pl.multiple_of(x * s.jy + (me ^ d) * s.jl, s.jl), s.jl)
                    for part in range(2):
                        rows = pl.ds(part * s.lx + first + x, s.jl, stride=2 * s.lx)
                        out_ref[rows, :] = held[at, part * LANES:(part + 1) * LANES]


def gather_modes(s, ins, gathered):
    me = lax.axis_index("planes")
    first = pl.program_id(1) * BLOCK
    for k, group in enumerate(ins):

        @pl.when(pl.program_id(0) == k)
        def _(group=group):
            for d, in_ref in enumerate(group):
                for x in range(BLOCK):
                    for part in range(2):
                        at = pl.ds(pl.multiple_of(part * s.jy + (me ^ d) * s.jl, s.jl), s.jl)
                        rows = pl.ds(part * s.lx + first + x, s.jl, stride=2 * s.lx)
                        gathered[x // 2, at, (x % 2) * LANES:(x % 2 + 1) * LANES] = in_ref[rows, :]


def by_group(s, refs):
    return [refs[k:k + s.planes] for k in range(0, len(refs), s.planes)]


def inverse_planes(s, gathered, second_ref, third_ref, planes):
    first = half_lanes((s.gy, LANES))
    sides = []
    for step in range(BLOCK // 2):
        out = square_dot(second_ref[...], gathered[step])
        for k in range(2):
            real = out[:s.gy, k * LANES:(k + 1) * LANES]
            imag = out[s.gy:, k * LANES:(k + 1) * LANES]
            for side in (
                jnp.where(first, real, pltpu.roll(imag, LANES // 2, 1)),
                jnp.where(first, pltpu.roll(real, LANES // 2, 1), imag),
            ):
                high, low = terms(side)
                sides.append(jnp.concatenate([high, low], 1))
    both = dot(jnp.concatenate(sides, 0), third_ref[...])
    planes[...] = both[:, :2 * s.gz] + both[:, 2 * s.gz:]


def plane_rows(s, row):
    return pl.ds(pl.multiple_of(row * s.gy, s.gy), s.gy)


def analysis_kernel(s, field_ref, third_ref, second_ref, outs, split, held):
    for x in range(BLOCK):
        for q in range(2):
            tile = jnp.concatenate([field_ref[0, 2 * q, x], field_ref[0, 2 * q + 1, x]], 1)
            place_terms(s, 2 * x + q, tile, split)
    forward_planes(s, split, third_ref, second_ref, held)
    scatter_modes(s, outs, held)


def middle_kernel(
    s, ins, point_ref, cot_ref, inv_second, inv_third, third_ref, second_ref,
    output_ref, grad_ref, outs, gathered, planes, split, held,
):
    gather_modes(s, ins, gathered)
    inverse_planes(s, gathered, inv_second, inv_third, planes)

    def one(x, carry):
        for q in range(2):
            grads = []
            for c in range(2):
                v = planes[plane_rows(s, 2 * x + q), c * s.gz:(c + 1) * s.gz] + point_ref[0, 2 * q + c, x]
                normal_cdf, slope = gelu_parts(v)
                output_ref[0, 2 * q + c, x] = v * normal_cdf
                grad = cot_ref[0, 2 * q + c, x] * slope
                grad_ref[0, 2 * q + c, x] = grad
                grads.append(grad)
            place_terms(s, 2 * x + q, jnp.concatenate(grads, 1), split)
        return carry

    lax.fori_loop(0, BLOCK, one, 0)
    forward_planes(s, split, third_ref, second_ref, held)
    scatter_modes(s, outs, held)


def final_kernel(s, ins, local_ref, inv_second, inv_third, out_ref, gathered, planes):
    gather_modes(s, ins, gathered)
    inverse_planes(s, gathered, inv_second, inv_third, planes)

    def one(x, carry):
        for q in range(2):
            for c in range(2):
                out_ref[0, 2 * q + c, x] = (
                    planes[plane_rows(s, 2 * x + q), c * s.gz:(c + 1) * s.gz] + local_ref[0, 2 * q + c, x]
                )
        return carry

    lax.fori_loop(0, BLOCK, one, 0)


def whole(array):
    rank = len(array.shape)
    return pl.BlockSpec(array.shape, lambda *_: (0,) * rank, pipeline_mode=pl.Buffered(1))


def cost(flops, *arrays):
    count = sum(int(np.prod(a.shape)) * a.dtype.itemsize for a in arrays)
    return pl.CostEstimate(flops=int(flops), bytes_accessed=count, transcendentals=0)


def anywhere():
    return pl.BlockSpec(memory_space=pl.ANY)


def chan_index():
    return lax.axis_index("chan").astype(jnp.int32).reshape(1)


def grid_spec(s, start):
    return pl.BlockSpec(
        (1, s.gw, BLOCK, s.gy, s.gz), lambda k, x, me: (0, me[0] ^ (start + k), x, 0, 0)
    )


def mode_shape(s):
    return jax.ShapeDtypeStruct((s.jl * 2 * s.lx, LANES), f32)


def forward_scratch(s):
    return [
        pltpu.VMEM((2 * BLOCK * 2 * s.gy, 2 * s.gz), bf16),
        pltpu.VMEM((BLOCK * s.jy, 2 * LANES), f32),
    ]


def inverse_scratch(s):
    return [
        pltpu.VMEM((BLOCK // 2, 2 * s.jy, 2 * LANES), f32),
        pltpu.VMEM((BLOCK * 2 * s.gy, 2 * s.gz), f32),
    ]


def group_call(s, groups, body, in_specs, out_specs, out_shape, scratch, aliases, estimate, operands):
    return pl.pallas_call(
        body,
        grid_spec=pltpu.PrefetchScalarGridSpec(
            num_scalar_prefetch=1,
            grid=(groups, s.lx // BLOCK),
            in_specs=in_specs,
            out_specs=out_specs,
            scratch_shapes=scratch,
        ),
        out_shape=out_shape,
        input_output_aliases=aliases,
        cost_estimate=estimate,
    )(chan_index(), *operands)


def analysis(s, field, second, third):
    tables = (third[0], second[0])
    out = mode_shape(s)
    count = 1 + len(tables)

    def body(me_ref, *refs):
        analysis_kernel(s, *refs[:count], by_group(s, refs[count:-2]), *refs[-2:])

    return by_group(s, group_call(
        s, s.chan, body,
        [grid_spec(s, 0)] + [whole(t) for t in tables],
        [whole(out)] * s.owners,
        [out] * s.owners,
        forward_scratch(s),
        {},
        cost(6e9, *[out] * 80),
        (field, *tables),
    ))


def middle(s, modes, point, cotangent, start, second, third, totals):
    tables = (second[1], third[1], third[0], second[0])
    out = mode_shape(s)
    spec = grid_spec(s, start)
    sources = len(modes)
    count = sources + 2 + len(tables)

    def body(me_ref, *refs):
        rest = refs[count + len(totals):]
        middle_kernel(
            s, by_group(s, refs[:sources]), *refs[sources:count], rest[0], rest[1],
            by_group(s, rest[2:-4]), *rest[-4:],
        )

    grid = jax.ShapeDtypeStruct(point.shape, f32)
    results = group_call(
        s, sources // s.planes, body,
        [whole(out)] * sources + [spec, spec] + [whole(t) for t in tables] + [anywhere()] * len(totals),
        [spec, spec] + [whole(out)] * sources,
        [grid, grid] + [out] * sources,
        inverse_scratch(s) + forward_scratch(s),
        {1 + count + i: i for i in range(len(totals))},
        cost(6e9, *[out] * 144),
        (*modes, point, cotangent, *tables, *totals),
    )
    return results[:2], by_group(s, results[2:])


def final(s, modes, local_grad, start, second, third, totals):
    tables = (second[1], third[1])
    out = mode_shape(s)
    spec = grid_spec(s, start)
    sources = len(modes)
    count = sources + 1 + len(tables)

    def body(me_ref, *refs):
        final_kernel(s, by_group(s, refs[:sources]), *refs[sources:count], *refs[count + len(totals):])

    return group_call(
        s, sources // s.planes, body,
        [whole(out)] * sources + [spec] + [whole(t) for t in tables] + [anywhere()] * len(totals),
        [spec],
        [jax.ShapeDtypeStruct(local_grad.shape, f32)],
        inverse_scratch(s),
        {1 + count + i: i for i in range(len(totals))},
        cost(3e9, *[out] * 72),
        (*modes, local_grad, *tables, *totals),
    )


def pointwise_kernel(values_ref, mixing_ref, bias_ref, out_ref):
    channels, strip = values_ref.shape[1], mixing_ref.shape[1] // values_ref.shape[1]
    rows = channels * strip

    def strips(step, carry):
        at = [pl.ds(pl.multiple_of((2 * step + k) * strip, strip), strip) for k in range(2)]
        value = jnp.concatenate([values_ref[0, :, 0, a, :].reshape(rows, LANES) for a in at], 1)
        high, low = terms(value)
        both = dot(mixing_ref[...], high)
        out = both[:rows] + both[rows:] + dot(mixing_ref[:rows, :], low)
        for k in range(2):
            one = out[:, k * LANES:(k + 1) * LANES] + bias_ref[...]
            out_ref[0, :, 0, at[k], :] = one.reshape(channels, strip, LANES)
        return carry

    lax.fori_loop(0, values_ref.shape[3] // (2 * strip), strips, 0, unroll=True)


def pointwise(values, weight, bias):
    _, channels, lx, gy, gz = values.shape
    strip = 2 * LANES // channels
    mixing = jnp.kron(weight.T, jnp.eye(strip, dtype=f32))
    high = lax.reduce_precision(mixing, 8, 7)
    mixing = jnp.concatenate([high.astype(bf16), (mixing - high).astype(bf16)], 0)
    bias_rows = jnp.broadcast_to(jnp.repeat(bias, strip)[:, None], (channels * strip, LANES))
    spec = pl.BlockSpec((1, channels, 1, gy, gz), lambda x: (0, 0, x, 0, 0))
    return pl.pallas_call(
        pointwise_kernel,
        grid=(lx,),
        in_specs=[spec, whole(mixing), whole(bias_rows)],
        out_specs=spec,
        out_shape=jax.ShapeDtypeStruct(values.shape, f32),
        cost_estimate=cost(6e9, values, values),
        name="pointwise",
    )(values, mixing, bias_rows)


def distances(s):
    return [(p, c) for p in range(s.planes) for c in range(s.chan)]


def owner_rows(s, p, c, step):
    owner = (lax.axis_index("planes") ^ p) * s.chan + (lax.axis_index("chan") ^ c)
    return pl.ds(pl.multiple_of(owner * step, step), step)


def first_kernel(s, ins, stacked_ref, outs, gathered, held):
    me = lax.axis_index("chan")
    rows = held.shape[0]
    per = 2 * s.lx
    for in_ref, (p, c) in zip(ins, distances(s)):
        for j in range(2):
            gathered[owner_rows(s, p, c, per), j * LANES:(j + 1) * LANES] = in_ref[j * per:(j + 1) * per, :]
    high, low = terms(gathered[...])
    both = dot(stacked_ref[...], high)
    held[...] = both[:rows] + both[rows:] + dot(stacked_ref[:rows, :], low)
    step = rows // s.chan
    for d, out_ref in enumerate(outs):
        at = pl.ds(pl.multiple_of((me ^ d) * step, step), step)
        for j in range(2):
            out_ref[j * step:(j + 1) * step, :] = held[at, j * LANES:(j + 1) * LANES]


def first_pass(s, arrived, table, mode_chunk, after):
    rows = table.shape[0]
    stacked = np.concatenate(two_terms(table), 0)
    pairs = s.jl // MODE_CHUNKS // 2
    out = jax.ShapeDtypeStruct((pairs * 2 * 2 * s.jxl, LANES), f32)
    offset = mode_chunk * pairs

    def body(*refs):
        outs = refs[s.owners + 1 + len(after):-2]
        first_kernel(s, refs[:s.owners], refs[s.owners], outs, *refs[-2:])

    return pl.pallas_call(
        body,
        grid=(pairs,),
        in_specs=[pl.BlockSpec((4 * s.lx, LANES), lambda j: (j + offset, 0))] * s.owners
        + [whole(stacked)]
        + [anywhere()] * len(after),
        out_specs=[pl.BlockSpec((4 * s.jxl, LANES), lambda j: (j, 0))] * s.chan,
        out_shape=[out] * s.chan,
        scratch_shapes=[
            pltpu.VMEM((s.owners * 2 * s.lx, 2 * LANES), f32),
            pltpu.VMEM((rows, 2 * LANES), f32),
        ],
        cost_estimate=cost(1e9 / MODE_CHUNKS, *[out] * 12),
        name="first_forward",
    )(*arrived, stacked, *after)


def back_kernel(s, ins, table_ref, outs, gathered, held):
    me = lax.axis_index("chan")
    step = 2 * s.jxl
    for d, in_ref in enumerate(ins):
        at = pl.ds(pl.multiple_of((me ^ d) * step, step), step)
        for j in range(2):
            gathered[at, j * LANES:(j + 1) * LANES] = in_ref[j * step:(j + 1) * step, :]
    held[...] = square_dot(table_ref[...], gathered[...])
    per = 2 * s.lx
    for out_ref, (p, c) in zip(outs, distances(s)):
        for j in range(2):
            out_ref[j * per:(j + 1) * per, :] = held[owner_rows(s, p, c, per), j * LANES:(j + 1) * LANES]


def first_inverse(s, modes, table, mode_chunk, totals):
    square = stacked_square(table)
    pairs = s.jl // MODE_CHUNKS // 2
    offset = mode_chunk * pairs
    out = mode_shape(s)
    count = s.chan + 1

    def body(*refs):
        back_kernel(s, refs[:s.chan], refs[s.chan], refs[count + len(totals):-2], *refs[-2:])

    return pl.pallas_call(
        body,
        grid=(pairs,),
        in_specs=[pl.BlockSpec((4 * s.jxl, LANES), lambda j: (j, 0))] * s.chan
        + [whole(square)]
        + [anywhere()] * len(totals),
        out_specs=[pl.BlockSpec((4 * s.lx, LANES), lambda j: (j + offset, 0))] * s.owners,
        out_shape=[out] * s.owners,
        scratch_shapes=[
            pltpu.VMEM((s.chan * 2 * s.jxl, 2 * LANES), f32),
            pltpu.VMEM((s.owners * 2 * s.lx, 2 * LANES), f32),
        ],
        input_output_aliases={count + i: i for i in range(len(totals))},
        cost_estimate=cost(1e9 / MODE_CHUNKS, *modes, *modes, *modes),
        name="first_inverse",
    )(*modes, square, *totals)


def swap_groups(pieces, width):
    count = len(pieces)
    lane = lax.broadcasted_iota(jnp.int32, pieces[0].shape, 1)
    step = count // 2
    pieces = list(pieces)
    while step:
        upper = (lane // (width * step)) % 2 == 1
        for a in range(count):
            if a & step:
                continue
            low, high = pieces[a], pieces[a + step]
            pieces[a] = jnp.where(upper, pltpu.roll(high, width * step, 1), low)
            pieces[a + step] = jnp.where(upper, high, pltpu.roll(low, LANES - width * step, 1))
        step //= 2
    return pieces


def spread_modes(s, count, ins, out_ref, factor=None):
    stride = 2 * s.jxl
    me = lax.axis_index("chan")
    for d, in_ref in enumerate(ins):
        for part in range(2):
            for a in range(s.jxl // s.gw):
                pieces = [
                    in_ref[pl.ds(part * s.jxl + a * s.gw + b, count, stride=stride), :]
                    for b in range(s.gw)
                ]
                for c, piece in enumerate(swap_groups(pieces, s.modes)):
                    if factor is not None:
                        piece = piece * factor
                    out_ref[part, (me ^ d) * s.gw + c, :, a * LANES:(a + 1) * LANES] = piece


def depth_factor(s, shape):
    lane = lax.broadcasted_iota(jnp.int32, shape, 1)
    return jnp.where(lane % s.modes == 0, s.scale, 2.0 * s.scale).astype(f32)


def store_block(s, count, block, outs, held):
    stride = 2 * s.jxl
    for part in range(2):
        for a in range(s.flat // LANES):
            for b, piece in enumerate(swap_groups([block[part][c][a] for c in range(s.gw)], s.modes)):
                held[pl.ds(part * s.jxl + a * s.gw + b, count, stride=stride), :] = piece
    for d, out_ref in enumerate(outs):

        @pl.when(pl.program_id(0) == d)
        def _(out_ref=out_ref):
            out_ref[...] = held[...]


def mix_kernel(s, count, adjoint, *refs):
    ins, weight_ref, outs = refs[1:1 + s.chan], refs[1 + s.chan], refs[2 + s.chan:2 + 2 * s.chan]
    kept_ref, held = refs[-2:]
    factor = depth_factor(s, (count, LANES))

    @pl.when(pl.program_id(0) == 0)
    def _():
        spread_modes(s, count, ins, kept_ref, factor if adjoint else None)

    pieces = s.flat // LANES
    block = [[[None] * pieces for _ in range(s.gw)] for _ in range(2)]
    for a in range(pieces):
        at = slice(a * LANES, (a + 1) * LANES)
        reals = [None] * s.gw
        imags = [None] * s.gw
        for i in range(s.ch):
            real = kept_ref[0, i, :, at]
            imag = kept_ref[1, i, :, at]
            for o in range(s.gw):
                pick = (o, i) if adjoint else (i, o)
                w_real = weight_ref[(0,) + pick + (slice(None), at)]
                w_imag = weight_ref[(1,) + pick + (slice(None), at)]
                if adjoint:
                    new_real = real * w_real + imag * w_imag
                    new_imag = imag * w_real - real * w_imag
                else:
                    new_real = real * w_real - imag * w_imag
                    new_imag = real * w_imag + imag * w_real
                reals[o] = new_real if i == 0 else reals[o] + new_real
                imags[o] = new_imag if i == 0 else imags[o] + new_imag
        for o in range(s.gw):
            block[0][o][a] = reals[o] if adjoint else reals[o] * factor
            block[1][o][a] = imags[o] if adjoint else imags[o] * factor
    store_block(s, count, block, outs, held)


def mix(s, modes, spec_weight, mode_chunk, adjoint):
    count = s.jl // MODE_CHUNKS
    kept_shape = jax.ShapeDtypeStruct((2, s.ch, count, s.flat), f32)
    me = chan_index()
    if adjoint:
        weights = pl.BlockSpec((2, s.gw, s.ch, count, s.flat), lambda d, me: (0, d ^ me[0], 0, mode_chunk, 0))
    else:
        weights = pl.BlockSpec((2, s.ch, s.gw, count, s.flat), lambda d, me: (0, 0, d ^ me[0], mode_chunk, 0))
    out = jax.ShapeDtypeStruct(modes[0].shape, f32)
    results = pl.pallas_call(
        functools.partial(mix_kernel, s, count, adjoint),
        grid_spec=pltpu.PrefetchScalarGridSpec(
            num_scalar_prefetch=1,
            grid=(s.chan,),
            in_specs=[whole(v) for v in modes] + [weights],
            out_specs=[whole(out)] * s.chan + [whole(kept_shape)],
            scratch_shapes=[pltpu.VMEM(out.shape, f32)],
        ),
        out_shape=[out] * s.chan + [kept_shape],
        cost_estimate=cost(1e8, *modes, *modes, *[kept_shape] * 8),
        name="unmix" if adjoint else "mix",
    )(me, *modes, spec_weight)
    return results[:s.chan], results[s.chan]


def weight_kernel(s, width, spec_ref, grad_ref, out_ref):
    for i in range(width):
        for a in range(s.flat // LANES):
            at = slice(a * LANES, (a + 1) * LANES)
            real = spec_ref[0, i, :, at]
            imag = spec_ref[1, i, :, at]
            for o in range(s.ch):
                g_real = grad_ref[0, o, :, at]
                g_imag = grad_ref[1, o, :, at]
                out_ref[0, i, o, :, at] = real * g_real + imag * g_imag
                out_ref[1, i, o, :, at] = real * g_imag - imag * g_real


def weight_grads(s, spec, grad, mode_chunk, total):
    count = s.jl // MODE_CHUNKS
    width = 2
    aliased = [] if total is None else [total]

    def body(spec_ref, grad_ref, *refs):
        weight_kernel(s, width, spec_ref, grad_ref, refs[-1])

    shape = jax.ShapeDtypeStruct((2, s.ch, s.ch, s.jl, s.flat), f32)
    return pl.pallas_call(
        body,
        grid=(s.ch // width,),
        in_specs=[pl.BlockSpec((2, width, count, s.flat), lambda i: (0, i, 0, 0)), whole(grad)]
        + [pl.BlockSpec(memory_space=pl.ANY)] * len(aliased),
        out_specs=pl.BlockSpec((2, width, s.ch, count, s.flat), lambda i: (0, i, 0, mode_chunk, 0)),
        out_shape=shape,
        input_output_aliases={2 + i: i for i in range(len(aliased))},
        cost_estimate=cost(1e8, shape),
        name="weight_grads",
    )(spec, grad, *aliased)


def over_owners(s, p, c, value):
    if p == 0 and c == 0:
        return value
    pairs = [(i, i ^ (p * s.chan + c)) for i in range(s.owners)]
    return lax.ppermute(value, ("planes", "chan"), pairs)


def over_chan(s, values):
    moved = [values[0]]
    for d in range(1, s.chan):
        moved.append(lax.ppermute(values[d], "chan", [(i, i ^ d) for i in range(s.chan)]))
    return moved


def mode_side(s, sent, tables, spec_weight, adjoint, after):
    mode_chunks = range(MODE_CHUNKS)
    arrived = [over_owners(s, p, c, sent[c][p]) for p, c in distances(s)]
    owned = []
    for m in mode_chunks:
        sent_on = first_pass(s, arrived, tables[0], m, after)
        after = sent_on[:1]
        owned.append(over_chan(s, sent_on))
    mixed = [mix(s, owned[m], spec_weight, m, adjoint) for m in mode_chunks]
    returned = [over_chan(s, v[0]) for v in mixed]
    totals = ()
    for m in mode_chunks:
        totals = first_inverse(s, returned[m], tables[1], m, totals)
    back = {d: over_owners(s, *d, value) for d, value in zip(distances(s), totals)}
    return back, [v[1] for v in mixed]


def fast_local(s, field, cotangent, spec_weight, point_weight, bias):
    second = second_tables(s)
    third = third_tables(s)
    first = first_tables(s)
    halves = [range(k, k + s.chan // 2) for k in (0, s.chan // 2)]
    sent = analysis(s, field, second, third)
    point = pointwise(field, point_weight, bias)
    back, spec_kept = mode_side(s, sent, first, spec_weight, False, (point,))
    totals, sent = (), []
    for half in halves:
        modes = [back[p, c] for c in half for p in range(s.planes)]
        totals, parts = middle(s, modes, point, cotangent, half[0], second, third, totals)
        sent += parts
    output, grad = totals
    local_grad = pointwise(grad, point_weight.T, jnp.zeros_like(bias))
    back, grad_kept = mode_side(s, sent, first, spec_weight, True, (local_grad,))
    weight_grad = None
    for m in range(MODE_CHUNKS):
        weight_grad = weight_grads(
            s, spec_kept[m], grad_kept[m], m, weight_grad
        )
    totals = ()
    for half in halves:
        modes = [back[p, c] for c in half for p in range(s.planes)]
        totals = final(s, modes, local_grad, half[0], second, third, totals)
    return output, totals[0], weight_grad


def local(field, cotangent, spec_weight, point_weight, bias):
    s = Sizes(field, spec_weight)
    if s.fits():
        return fast_local(s, field, cotangent, spec_weight, point_weight, bias)
    return plain_local(s, field, cotangent, spec_weight, point_weight, bias)


def solution(mesh):
    in_specs = (
        P("groups", None, ("planes", "chan"), None, None),
        P("groups", None, ("planes", "chan"), None, None),
        P(None, None, None, "planes", "chan"),
        P(),
        P(),
    )
    out_specs = (
        P("groups", None, ("planes", "chan"), None, None),
        P("groups", None, ("planes", "chan"), None, None),
        P("groups", None, None, "planes", "chan"),
    )
    return jax.shard_map(local, mesh=mesh, in_specs=in_specs, out_specs=out_specs, check_vma=False)
```

```python
import functools
import math

import numpy as np

import jax
import jax.numpy as jnp
from jax import lax
from jax.experimental import pallas as pl
from jax.experimental.pallas import tpu as pltpu
from jax.sharding import PartitionSpec as P


exact_mode = lax.Precision.HIGHEST


def retained(s, length):
    indices = jnp.arange(2 * s.modes)
    return jnp.where(indices < s.modes, indices, length - 2 * s.modes + indices)


def phase_table(positions, freqs, length):
    turn_count = positions[:, None] * freqs[None, :] % length
    angles = turn_count.astype(jnp.float32) * (2.0 * math.pi / length)
    return (jnp.cos(angles), jnp.sin(angles))


def plain_analysis(s, field):
    batch_size, channels, local_planes, second_length, third_length = field.shape
    plane_count = lax.axis_size("planes")
    channel_groups = lax.axis_size("chan")
    group_width = channels // channel_groups
    local_modes = 2 * s.modes // plane_count
    first_length = local_planes * plane_count * channel_groups
    cosine, sine_part = phase_table(
        jnp.arange(second_length), retained(s, second_length), second_length
    )
    second_table = jnp.stack([cosine, -sine_part], 1).reshape(
        second_length, 2, plane_count, local_modes
    )
    cosine, sine_part = phase_table(jnp.arange(third_length), jnp.arange(s.modes), third_length)
    third_table = jnp.stack(
        [jnp.stack([cosine, -sine_part], 1), jnp.stack([sine_part, cosine], 1)], 0
    )
    grouped = field.reshape(
        batch_size, channel_groups, group_width, local_planes, second_length, third_length
    )
    second_pass = jnp.einsum("bcdxyz,yspk->bcdxspkz", grouped, second_table, precision=exact_mode)
    spectra = jnp.einsum("bcdxspkz,sztm->bpckxdtm", second_pass, third_table, precision=exact_mode)
    spectra = spectra.reshape(
        batch_size, plane_count * channel_groups, local_modes, local_planes, group_width * 2 * s.modes
    )
    arrived = lax.all_to_all(spectra, ("planes", "chan"), split_axis=1, concat_axis=3, tiled=True)
    positions = jnp.arange(first_length)
    arrived = arrived.reshape(batch_size, local_modes, first_length, group_width, 2, s.modes)
    cosine, sine_part = phase_table(positions, retained(s, first_length), first_length)
    first_table = jnp.stack(
        [jnp.stack([cosine, -sine_part], 1), jnp.stack([sine_part, cosine], 1)], 1
    )
    first_pass = jnp.einsum("bkxdsm,xstf->bkdtfm", arrived, first_table, precision=exact_mode)
    first_pass = first_pass.reshape(batch_size, local_modes, group_width, 2, 2 * s.modes * s.modes)
    return lax.all_to_all(first_pass, "chan", split_axis=4, concat_axis=2, tiled=True)


def plain_synthesis(s, spectrum):
    batch_size, local_modes, channels = (spectrum.shape[0], spectrum.shape[1], spectrum.shape[2])
    plane_count = lax.axis_size("planes")
    channel_groups = lax.axis_size("chan")
    group_width = channels // channel_groups
    local_planes = s.gx // (plane_count * channel_groups)
    gathered = lax.all_to_all(spectrum, "chan", split_axis=2, concat_axis=4, tiled=True)
    gathered = gathered.reshape(batch_size, local_modes, group_width, 2, 2 * s.modes, s.modes)
    cosine, sine_part = phase_table(jnp.arange(s.gx), retained(s, s.gx), s.gx)
    cosine_t = cosine.T
    sine_t = sine_part.T
    first_inverse = jnp.stack(
        [jnp.stack([cosine_t, sine_t], -1), jnp.stack([-sine_t, cosine_t], -1)], 0
    )
    first_pass = jnp.einsum("bkdsfm,sfxt->bkxdtm", gathered, first_inverse, precision=exact_mode)
    first_pass = first_pass.reshape(batch_size, local_modes, s.gx, group_width * 2 * s.modes)
    returned = lax.all_to_all(
        first_pass[:, None], ("planes", "chan"), split_axis=3, concat_axis=1, tiled=True
    )
    returned = returned.reshape(
        batch_size, plane_count, channel_groups, local_modes, local_planes, group_width, 2, s.modes
    )
    source_form = "bpckxdtm"
    cosine, sine_part = phase_table(jnp.arange(s.gz), jnp.arange(s.modes), s.gz)
    cosine_t = cosine.T
    sine_t = sine_part.T
    third_inverse = jnp.stack(
        [jnp.stack([cosine_t, sine_t], 1), jnp.stack([-sine_t, cosine_t], 1)], 0
    )
    depth_pass = jnp.einsum(
        source_form + ",tmuz->bcdxpkuz", returned, third_inverse, precision=exact_mode
    )
    cosine, sine_part = phase_table(jnp.arange(s.gy), retained(s, s.gy), s.gy)
    second_inverse = jnp.stack([cosine.T, -sine_part.T], 0).reshape(2, plane_count, local_modes, s.gy)
    physical = jnp.einsum("bcdxpkuz,upky->bcdxyz", depth_pass, second_inverse, precision=exact_mode)
    return physical.reshape(batch_size, channels, local_planes, s.gy, s.gz)


def mode_weighting(s, mode_count):
    depth_mode = jnp.arange(mode_count) % s.modes
    return jnp.where(depth_mode == 0, 1.0, 2.0).astype(jnp.float32) / float(s.gx * s.gy * s.gz)


def contract(operand, weights):
    return jnp.einsum("bkin,iokn->bkon", operand, weights, precision=exact_mode)


def adjoint(operand, weights):
    return jnp.einsum("bkon,iokn->bkin", operand, weights, precision=exact_mode)


def outer_sum(first_operand, second_operand):
    return jnp.einsum("bkin,bkon->iokn", first_operand, second_operand, precision=exact_mode)


def plain_local(s, field, cotangent, spec_weight, point_weight, bias):
    spectrum = plain_analysis(s, field)
    weight_re = spec_weight[0]
    weight_im = spec_weight[1]
    spec_re = spectrum[:, :, :, 0]
    spec_im = spectrum[:, :, :, 1]
    weighting = mode_weighting(s, spectrum.shape[-1])
    mixed_re = (contract(spec_re, weight_re) - contract(spec_im, weight_im)) * weighting
    mixed_im = (contract(spec_re, weight_im) + contract(spec_im, weight_re)) * weighting
    mixed_modes = jnp.stack([mixed_re, mixed_im], 3)
    spectral = plain_synthesis(s, mixed_modes)
    pointwise = jnp.einsum("bixyz,io->boxyz", field, point_weight, precision=exact_mode)
    preactivation = spectral + pointwise + bias[None, :, None, None, None]
    normal_cdf = 0.5 * (1.0 + lax.erf(preactivation * (1.0 / math.sqrt(2.0))))
    output = preactivation * normal_cdf
    derivative = normal_cdf + preactivation * jnp.exp(-0.5 * preactivation * preactivation) * (
        1.0 / math.sqrt(2.0 * math.pi)
    )
    pre_grad = cotangent * derivative
    raw_grad = plain_analysis(s, pre_grad)
    grad_re = raw_grad[:, :, :, 0] * weighting
    grad_im = raw_grad[:, :, :, 1] * weighting
    spectrum_grad = jnp.stack(
        [
            adjoint(grad_re, weight_re) + adjoint(grad_im, weight_im),
            adjoint(grad_im, weight_re) - adjoint(grad_re, weight_im),
        ],
        3,
    )
    weight_grad = jnp.stack(
        [
            outer_sum(spec_re, grad_re) + outer_sum(spec_im, grad_im),
            outer_sum(spec_re, grad_im) - outer_sum(spec_im, grad_re),
        ],
        0,
    )
    local_grad = jnp.einsum("boxyz,io->bixyz", pre_grad, point_weight, precision=exact_mode)
    field_grad = local_grad + plain_synthesis(s, spectrum_grad)
    return (output, field_grad, weight_grad)


LANES = 128
BLOCK = 4
MODE_CHUNKS = 2
f32 = jnp.float32
bf16 = jnp.bfloat16


class Sizes:
    def __init__(self, field, spec_weight):
        self.planes = lax.axis_size("planes")
        self.chan = lax.axis_size("chan")
        self.owners = self.planes * self.chan
        _, self.ch, self.lx, self.gy, self.gz = field.shape
        self.gx = self.lx * self.owners
        _, _, _, self.jl, local_flat = spec_weight.shape
        self.jy = self.jl * self.planes
        self.flat = local_flat
        self.modes = self.jy // 2
        self.jxl = local_flat // self.modes
        self.jx = self.jxl * self.chan
        self.gw = self.ch // self.chan
        self.scale = 1.0 / float(self.gx * self.gy * self.gz)

    def fits(self):
        return (
            self.gw == 4
            and self.gw * self.modes == LANES
            and self.gz == LANES
            and self.gy == LANES
            and self.jy * 2 == LANES
            and self.jx * 2 == LANES
            and self.flat % LANES == 0
            and self.ch * 16 == 2 * LANES
            and self.jl % (8 * MODE_CHUNKS) == 0
            and self.lx % (2 * BLOCK) == 0
            and self.gx == LANES
            and self.chan & (self.chan - 1) == 0
            and self.planes & (self.planes - 1) == 0
        )


def kept(count, length):
    index = np.arange(count)
    return np.where(index < count // 2, index, length - count + index)


def waves(freqs, length):
    turns = (freqs[:, None] * np.arange(length)[None, :]) % length
    angles = turns * (2.0 * math.pi / length)
    return np.cos(angles), np.sin(angles)


def two_terms(table):
    table = np.asarray(table, np.float32)
    high = table.astype(jnp.bfloat16)
    low = (table - high.astype(np.float32)).astype(jnp.bfloat16)
    return high, low


def stacked_square(table):
    high, low = two_terms(table)
    return np.concatenate([np.concatenate([high, high], 1), np.concatenate([low, low], 1)], 0)


def second_tables(s):
    cosine, sine = waves(kept(s.jy, s.gy), s.gy)
    forward = np.concatenate([cosine, sine], 0)
    inverse = np.concatenate(
        [np.concatenate([cosine.T, -sine.T], 1), np.concatenate([sine.T, cosine.T], 1)], 0
    )
    return stacked_square(forward), stacked_square(inverse)


def third_tables(s):
    cosine, sine = waves(np.arange(s.modes), s.gz)
    table = np.zeros((2, s.gz, 2, 2, s.modes))
    for c in range(2):
        table[c, :, 0, c] = cosine.T
        table[c, :, 1, c] = -sine.T
    table = table.reshape(2 * s.gz, LANES)
    forward = np.concatenate(two_terms(table), 1)
    high, low = two_terms(table.T)
    wide = np.concatenate([high, low], 1)
    return forward, np.concatenate([wide, wide], 0)


def first_tables(s):
    cosine, sine = waves(kept(s.jx, s.gx), s.gx)
    c4 = cosine.reshape(s.chan, s.jxl, s.owners, s.lx)
    s4 = sine.reshape(s.chan, s.jxl, s.owners, s.lx)
    forward = np.zeros((s.chan, 2, s.jxl, s.owners, 2, s.lx))
    inverse = np.zeros((s.owners, 2, s.lx, s.chan, 2, s.jxl))
    for out, inp, sign, wave in ((0, 0, 1, c4), (0, 1, 1, s4), (1, 0, -1, s4), (1, 1, 1, c4)):
        forward[:, out, :, :, inp] = sign * wave
        inverse[:, inp, :, :, out] = sign * wave.transpose(2, 3, 0, 1)
    rows = s.chan * 2 * s.jxl
    return forward.reshape(rows, -1), inverse.reshape(-1, rows)


def terms(value):
    high = value.astype(bf16)
    return high, (value - high.astype(f32)).astype(bf16)


def dot(a, b):
    return jnp.dot(a, b, preferred_element_type=f32)


def square_dot(table, value):
    high, low = terms(value)
    both = dot(table, jnp.concatenate([high, low], 0))
    half = both.shape[0] // 2
    return both[:half] + both[half:]


def gelu_parts(v):
    normal_cdf = 0.5 * (1.0 + lax.erf(v * (1.0 / math.sqrt(2.0))))
    slope = normal_cdf + v * jnp.exp(-0.5 * v * v) * (1.0 / math.sqrt(2.0 * math.pi))
    return normal_cdf, slope


def half_lanes(shape):
    return lax.broadcasted_iota(jnp.int32, shape, 1) < LANES // 2


def place_terms(s, row, value, split):
    half = split.shape[0] // 2
    high, low = terms(value)
    split[pl.ds(pl.multiple_of(row * s.gy, s.gy), s.gy), :] = high
    split[pl.ds(pl.multiple_of(half + row * s.gy, s.gy), s.gy), :] = low


def forward_planes(s, split, third_ref, second_ref, held):
    half = split.shape[0] // 2
    both = dot(split[...], third_ref[...])
    deep = both[:half, :LANES] + both[:half, LANES:] + both[half:, :LANES]
    first = half_lanes((s.jy, LANES))
    for x in range(BLOCK):
        side = [deep[(2 * x + q) * s.gy:(2 * x + q + 1) * s.gy] for q in range(2)]
        out = square_dot(second_ref[...], jnp.concatenate(side, 1))
        pairs = []
        for k in range(2):
            turned = pltpu.roll(out[s.jy:, k * LANES:(k + 1) * LANES], LANES // 2, 1)
            pairs.append(out[:s.jy, k * LANES:(k + 1) * LANES] + jnp.where(first, turned, -turned))
        rows = slice(x * s.jy, (x + 1) * s.jy)
        held[rows, :LANES] = jnp.where(first, pairs[0], pltpu.roll(pairs[1], LANES // 2, 1))
        held[rows, LANES:] = jnp.where(first, pltpu.roll(pairs[0], LANES // 2, 1), pairs[1])


def scatter_modes(s, outs, held):
    me = lax.axis_index("planes")
    first = pl.program_id(1) * BLOCK
    for k, group in enumerate(outs):

        @pl.when(pl.program_id(0) == k)
        def _(group=group):
            for d, out_ref in enumerate(group):
                for x in range(BLOCK):
                    at = pl.ds(pl.multiple_of(x * s.jy + (me ^ d) * s.jl, s.jl), s.jl)
                    for part in range(2):
                        rows = pl.ds(part * s.lx + first + x, s.jl, stride=2 * s.lx)
                        out_ref[rows, :] = held[at, part * LANES:(part + 1) * LANES]


def gather_modes(s, ins, gathered):
    me = lax.axis_index("planes")
    first = pl.program_id(1) * BLOCK
    for k, group in enumerate(ins):

        @pl.when(pl.program_id(0) == k)
        def _(group=group):
            for d, in_ref in enumerate(group):
                for x in range(BLOCK):
                    for part in range(2):
                        at = pl.ds(pl.multiple_of(part * s.jy + (me ^ d) * s.jl, s.jl), s.jl)
                        rows = pl.ds(part * s.lx + first + x, s.jl, stride=2 * s.lx)
                        gathered[x // 2, at, (x % 2) * LANES:(x % 2 + 1) * LANES] = in_ref[rows, :]


def by_group(s, refs):
    return [refs[k:k + s.planes] for k in range(0, len(refs), s.planes)]


def inverse_planes(s, gathered, second_ref, third_ref, planes):
    first = half_lanes((s.gy, LANES))
    sides = []
    for step in range(BLOCK // 2):
        out = square_dot(second_ref[...], gathered[step])
        for k in range(2):
            real = out[:s.gy, k * LANES:(k + 1) * LANES]
            imag = out[s.gy:, k * LANES:(k + 1) * LANES]
            for side in (
                jnp.where(first, real, pltpu.roll(imag, LANES // 2, 1)),
                jnp.where(first, pltpu.roll(real, LANES // 2, 1), imag),
            ):
                high, low = terms(side)
                sides.append(jnp.concatenate([high, low], 1))
    both = dot(jnp.concatenate(sides, 0), third_ref[...])
    planes[...] = both[:, :2 * s.gz] + both[:, 2 * s.gz:]


def plane_rows(s, row):
    return pl.ds(pl.multiple_of(row * s.gy, s.gy), s.gy)


def analysis_kernel(s, field_ref, third_ref, second_ref, outs, split, held):
    for x in range(BLOCK):
        for q in range(2):
            tile = jnp.concatenate([field_ref[0, 2 * q, x], field_ref[0, 2 * q + 1, x]], 1)
            place_terms(s, 2 * x + q, tile, split)
    forward_planes(s, split, third_ref, second_ref, held)
    scatter_modes(s, outs, held)


def middle_kernel(
    s, ins, point_ref, cot_ref, inv_second, inv_third, third_ref, second_ref,
    output_ref, grad_ref, outs, gathered, planes, split, held,
):
    gather_modes(s, ins, gathered)
    inverse_planes(s, gathered, inv_second, inv_third, planes)

    def one(x, carry):
        for q in range(2):
            grads = []
            for c in range(2):
                v = planes[plane_rows(s, 2 * x + q), c * s.gz:(c + 1) * s.gz] + point_ref[0, 2 * q + c, x]
                normal_cdf, slope = gelu_parts(v)
                output_ref[0, 2 * q + c, x] = v * normal_cdf
                grad = cot_ref[0, 2 * q + c, x] * slope
                grad_ref[0, 2 * q + c, x] = grad
                grads.append(grad)
            place_terms(s, 2 * x + q, jnp.concatenate(grads, 1), split)
        return carry

    lax.fori_loop(0, BLOCK, one, 0)
    forward_planes(s, split, third_ref, second_ref, held)
    scatter_modes(s, outs, held)


def final_kernel(s, ins, local_ref, inv_second, inv_third, out_ref, gathered, planes):
    gather_modes(s, ins, gathered)
    inverse_planes(s, gathered, inv_second, inv_third, planes)

    def one(x, carry):
        for q in range(2):
            for c in range(2):
                out_ref[0, 2 * q + c, x] = (
                    planes[plane_rows(s, 2 * x + q), c * s.gz:(c + 1) * s.gz] + local_ref[0, 2 * q + c, x]
                )
        return carry

    lax.fori_loop(0, BLOCK, one, 0)


def whole(array):
    rank = len(array.shape)
    return pl.BlockSpec(array.shape, lambda *_: (0,) * rank, pipeline_mode=pl.Buffered(1))


def cost(flops, *arrays):
    count = sum(int(np.prod(a.shape)) * a.dtype.itemsize for a in arrays)
    return pl.CostEstimate(flops=int(flops), bytes_accessed=count, transcendentals=0)


def anywhere():
    return pl.BlockSpec(memory_space=pl.ANY)


def chan_index():
    return lax.axis_index("chan").astype(jnp.int32).reshape(1)


def grid_spec(s, start, step=1):
    return pl.BlockSpec(
        (1, s.gw, BLOCK, s.gy, s.gz), lambda k, x, me: (0, me[0] ^ (start + step * k), x, 0, 0)
    )


def mode_shape(s):
    return jax.ShapeDtypeStruct((s.jl * 2 * s.lx, LANES), f32)


def forward_scratch(s):
    return [
        pltpu.VMEM((2 * BLOCK * 2 * s.gy, 2 * s.gz), bf16),
        pltpu.VMEM((BLOCK * s.jy, 2 * LANES), f32),
    ]


def inverse_scratch(s):
    return [
        pltpu.VMEM((BLOCK // 2, 2 * s.jy, 2 * LANES), f32),
        pltpu.VMEM((BLOCK * 2 * s.gy, 2 * s.gz), f32),
    ]


def group_call(s, groups, body, in_specs, out_specs, out_shape, scratch, aliases, estimate, operands):
    return pl.pallas_call(
        body,
        grid_spec=pltpu.PrefetchScalarGridSpec(
            num_scalar_prefetch=1,
            grid=(groups, s.lx // BLOCK),
            in_specs=in_specs,
            out_specs=out_specs,
            scratch_shapes=scratch,
        ),
        out_shape=out_shape,
        input_output_aliases=aliases,
        cost_estimate=estimate,
    )(chan_index(), *operands)


def analysis(s, field, start, step, second, third, after):
    tables = (third[0], second[0])
    out = mode_shape(s)
    count = 1 + len(tables)

    def body(me_ref, *refs):
        outs = by_group(s, refs[count + len(after):-2])
        analysis_kernel(s, *refs[:count], outs, *refs[-2:])

    return by_group(s, group_call(
        s, s.chan // 2, body,
        [grid_spec(s, start, step)] + [whole(t) for t in tables] + [anywhere()] * len(after),
        [whole(out)] * (s.owners // 2),
        [out] * (s.owners // 2),
        forward_scratch(s),
        {},
        cost(3e9, *[out] * 40),
        (field, *tables, *after),
    ))


def middle(s, modes, point, cotangent, start, second, third, totals):
    tables = (second[1], third[1], third[0], second[0])
    out = mode_shape(s)
    spec = grid_spec(s, start)
    sources = len(modes)
    count = sources + 2 + len(tables)

    def body(me_ref, *refs):
        rest = refs[count + len(totals):]
        middle_kernel(
            s, by_group(s, refs[:sources]), *refs[sources:count], rest[0], rest[1],
            by_group(s, rest[2:-4]), *rest[-4:],
        )

    grid = jax.ShapeDtypeStruct(point.shape, f32)
    results = group_call(
        s, sources // s.planes, body,
        [whole(out)] * sources + [spec, spec] + [whole(t) for t in tables] + [anywhere()] * len(totals),
        [spec, spec] + [whole(out)] * sources,
        [grid, grid] + [out] * sources,
        inverse_scratch(s) + forward_scratch(s),
        {1 + count + i: i for i in range(len(totals))},
        cost(6e9, *[out] * 144),
        (*modes, point, cotangent, *tables, *totals),
    )
    return results[:2], by_group(s, results[2:])


def final(s, modes, local_grad, start, second, third, totals):
    tables = (second[1], third[1])
    out = mode_shape(s)
    spec = grid_spec(s, start)
    sources = len(modes)
    count = sources + 1 + len(tables)

    def body(me_ref, *refs):
        final_kernel(s, by_group(s, refs[:sources]), *refs[sources:count], *refs[count + len(totals):])

    return group_call(
        s, sources // s.planes, body,
        [whole(out)] * sources + [spec] + [whole(t) for t in tables] + [anywhere()] * len(totals),
        [spec],
        [jax.ShapeDtypeStruct(local_grad.shape, f32)],
        inverse_scratch(s),
        {1 + count + i: i for i in range(len(totals))},
        cost(3e9, *[out] * 72),
        (*modes, local_grad, *tables, *totals),
    )


def pointwise_kernel(values_ref, mixing_ref, bias_ref, out_ref):
    channels, strip = values_ref.shape[1], mixing_ref.shape[1] // values_ref.shape[1]
    rows = channels * strip

    def strips(step, carry):
        at = [pl.ds(pl.multiple_of((2 * step + k) * strip, strip), strip) for k in range(2)]
        value = jnp.concatenate([values_ref[0, :, 0, a, :].reshape(rows, LANES) for a in at], 1)
        high, low = terms(value)
        both = dot(mixing_ref[...], high)
        out = both[:rows] + both[rows:] + dot(mixing_ref[:rows, :], low)
        for k in range(2):
            one = out[:, k * LANES:(k + 1) * LANES] + bias_ref[...]
            out_ref[0, :, 0, at[k], :] = one.reshape(channels, strip, LANES)
        return carry

    lax.fori_loop(0, values_ref.shape[3] // (2 * strip), strips, 0, unroll=True)


def pointwise(values, weight, bias):
    _, channels, lx, gy, gz = values.shape
    strip = 2 * LANES // channels
    mixing = jnp.kron(weight.T, jnp.eye(strip, dtype=f32))
    high = lax.reduce_precision(mixing, 8, 7)
    mixing = jnp.concatenate([high.astype(bf16), (mixing - high).astype(bf16)], 0)
    bias_rows = jnp.broadcast_to(jnp.repeat(bias, strip)[:, None], (channels * strip, LANES))
    spec = pl.BlockSpec((1, channels, 1, gy, gz), lambda x: (0, 0, x, 0, 0))
    return pl.pallas_call(
        pointwise_kernel,
        grid=(lx,),
        in_specs=[spec, whole(mixing), whole(bias_rows)],
        out_specs=spec,
        out_shape=jax.ShapeDtypeStruct(values.shape, f32),
        cost_estimate=cost(6e9, values, values),
        name="pointwise",
    )(values, mixing, bias_rows)


def distances(s):
    return [(p, c) for p in range(s.planes) for c in range(s.chan)]


def owner_rows(s, p, c, step):
    owner = (lax.axis_index("planes") ^ p) * s.chan + (lax.axis_index("chan") ^ c)
    return pl.ds(pl.multiple_of(owner * step, step), step)


def first_kernel(s, ins, stacked_ref, outs, gathered, held):
    me = lax.axis_index("chan")
    rows = held.shape[0]
    per = 2 * s.lx
    for in_ref, (p, c) in zip(ins, distances(s)):
        for j in range(2):
            gathered[owner_rows(s, p, c, per), j * LANES:(j + 1) * LANES] = in_ref[j * per:(j + 1) * per, :]
    high, low = terms(gathered[...])
    both = dot(stacked_ref[...], high)
    held[...] = both[:rows] + both[rows:] + dot(stacked_ref[:rows, :], low)
    step = rows // s.chan
    for d, out_ref in enumerate(outs):
        at = pl.ds(pl.multiple_of((me ^ d) * step, step), step)
        for j in range(2):
            out_ref[j * step:(j + 1) * step, :] = held[at, j * LANES:(j + 1) * LANES]


def first_pass(s, arrived, table, mode_chunk, after):
    rows = table.shape[0]
    stacked = np.concatenate(two_terms(table), 0)
    pairs = s.jl // MODE_CHUNKS // 2
    out = jax.ShapeDtypeStruct((pairs * 2 * 2 * s.jxl, LANES), f32)
    offset = mode_chunk * pairs

    def body(*refs):
        outs = refs[s.owners + 1 + len(after):-2]
        first_kernel(s, refs[:s.owners], refs[s.owners], outs, *refs[-2:])

    return pl.pallas_call(
        body,
        grid=(pairs,),
        in_specs=[pl.BlockSpec((4 * s.lx, LANES), lambda j: (j + offset, 0))] * s.owners
        + [whole(stacked)]
        + [anywhere()] * len(after),
        out_specs=[pl.BlockSpec((4 * s.jxl, LANES), lambda j: (j, 0))] * s.chan,
        out_shape=[out] * s.chan,
        scratch_shapes=[
            pltpu.VMEM((s.owners * 2 * s.lx, 2 * LANES), f32),
            pltpu.VMEM((rows, 2 * LANES), f32),
        ],
        cost_estimate=cost(1e9 / MODE_CHUNKS, *[out] * 12),
        name="first_forward",
    )(*arrived, stacked, *after)


def back_kernel(s, ins, table_ref, outs, gathered, held):
    me = lax.axis_index("chan")
    step = 2 * s.jxl
    for d, in_ref in enumerate(ins):
        at = pl.ds(pl.multiple_of((me ^ d) * step, step), step)
        for j in range(2):
            gathered[at, j * LANES:(j + 1) * LANES] = in_ref[j * step:(j + 1) * step, :]
    held[...] = square_dot(table_ref[...], gathered[...])
    per = 2 * s.lx
    for out_ref, (p, c) in zip(outs, distances(s)):
        for j in range(2):
            out_ref[j * per:(j + 1) * per, :] = held[owner_rows(s, p, c, per), j * LANES:(j + 1) * LANES]


def first_inverse(s, modes, table, mode_chunk, totals):
    square = stacked_square(table)
    pairs = s.jl // MODE_CHUNKS // 2
    offset = mode_chunk * pairs
    out = mode_shape(s)
    count = s.chan + 1

    def body(*refs):
        back_kernel(s, refs[:s.chan], refs[s.chan], refs[count + len(totals):-2], *refs[-2:])

    return pl.pallas_call(
        body,
        grid=(pairs,),
        in_specs=[pl.BlockSpec((4 * s.jxl, LANES), lambda j: (j, 0))] * s.chan
        + [whole(square)]
        + [anywhere()] * len(totals),
        out_specs=[pl.BlockSpec((4 * s.lx, LANES), lambda j: (j + offset, 0))] * s.owners,
        out_shape=[out] * s.owners,
        scratch_shapes=[
            pltpu.VMEM((s.chan * 2 * s.jxl, 2 * LANES), f32),
            pltpu.VMEM((s.owners * 2 * s.lx, 2 * LANES), f32),
        ],
        input_output_aliases={count + i: i for i in range(len(totals))},
        cost_estimate=cost(1e9 / MODE_CHUNKS, *modes, *modes, *modes),
        name="first_inverse",
    )(*modes, square, *totals)


def swap_groups(pieces, width):
    count = len(pieces)
    lane = lax.broadcasted_iota(jnp.int32, pieces[0].shape, 1)
    step = count // 2
    pieces = list(pieces)
    while step:
        upper = (lane // (width * step)) % 2 == 1
        for a in range(count):
            if a & step:
                continue
            low, high = pieces[a], pieces[a + step]
            pieces[a] = jnp.where(upper, pltpu.roll(high, width * step, 1), low)
            pieces[a + step] = jnp.where(upper, high, pltpu.roll(low, LANES - width * step, 1))
        step //= 2
    return pieces


def spread_modes(s, count, ins, out_ref, factor=None):
    stride = 2 * s.jxl
    me = lax.axis_index("chan")
    for d, in_ref in enumerate(ins):
        for part in range(2):
            for a in range(s.jxl // s.gw):
                pieces = [
                    in_ref[pl.ds(part * s.jxl + a * s.gw + b, count, stride=stride), :]
                    for b in range(s.gw)
                ]
                for c, piece in enumerate(swap_groups(pieces, s.modes)):
                    if factor is not None:
                        piece = piece * factor
                    out_ref[part, (me ^ d) * s.gw + c, :, a * LANES:(a + 1) * LANES] = piece


def depth_factor(s, shape):
    lane = lax.broadcasted_iota(jnp.int32, shape, 1)
    return jnp.where(lane % s.modes == 0, s.scale, 2.0 * s.scale).astype(f32)


def store_block(s, count, block, outs, held):
    stride = 2 * s.jxl
    for part in range(2):
        for a in range(s.flat // LANES):
            for b, piece in enumerate(swap_groups([block[part][c][a] for c in range(s.gw)], s.modes)):
                held[pl.ds(part * s.jxl + a * s.gw + b, count, stride=stride), :] = piece
    for d, out_ref in enumerate(outs):

        @pl.when(pl.program_id(0) == d)
        def _(out_ref=out_ref):
            out_ref[...] = held[...]


def mix_kernel(s, count, adjoint, *refs):
    ins, weight_ref, outs = refs[1:1 + s.chan], refs[1 + s.chan], refs[2 + s.chan:2 + 2 * s.chan]
    kept_ref, held = refs[-2:]
    factor = depth_factor(s, (count, LANES))

    @pl.when(pl.program_id(0) == 0)
    def _():
        spread_modes(s, count, ins, kept_ref, factor if adjoint else None)

    pieces = s.flat // LANES
    block = [[[None] * pieces for _ in range(s.gw)] for _ in range(2)]
    for a in range(pieces):
        at = slice(a * LANES, (a + 1) * LANES)
        reals = [None] * s.gw
        imags = [None] * s.gw
        for i in range(s.ch):
            real = kept_ref[0, i, :, at]
            imag = kept_ref[1, i, :, at]
            for o in range(s.gw):
                pick = (o, i) if adjoint else (i, o)
                w_real = weight_ref[(0,) + pick + (slice(None), at)]
                w_imag = weight_ref[(1,) + pick + (slice(None), at)]
                if adjoint:
                    new_real = real * w_real + imag * w_imag
                    new_imag = imag * w_real - real * w_imag
                else:
                    new_real = real * w_real - imag * w_imag
                    new_imag = real * w_imag + imag * w_real
                reals[o] = new_real if i == 0 else reals[o] + new_real
                imags[o] = new_imag if i == 0 else imags[o] + new_imag
        for o in range(s.gw):
            block[0][o][a] = reals[o] if adjoint else reals[o] * factor
            block[1][o][a] = imags[o] if adjoint else imags[o] * factor
    store_block(s, count, block, outs, held)


def mix(s, modes, spec_weight, mode_chunk, adjoint):
    count = s.jl // MODE_CHUNKS
    kept_shape = jax.ShapeDtypeStruct((2, s.ch, count, s.flat), f32)
    me = chan_index()
    if adjoint:
        weights = pl.BlockSpec((2, s.gw, s.ch, count, s.flat), lambda d, me: (0, d ^ me[0], 0, mode_chunk, 0))
    else:
        weights = pl.BlockSpec((2, s.ch, s.gw, count, s.flat), lambda d, me: (0, 0, d ^ me[0], mode_chunk, 0))
    out = jax.ShapeDtypeStruct(modes[0].shape, f32)
    results = pl.pallas_call(
        functools.partial(mix_kernel, s, count, adjoint),
        grid_spec=pltpu.PrefetchScalarGridSpec(
            num_scalar_prefetch=1,
            grid=(s.chan,),
            in_specs=[whole(v) for v in modes] + [weights],
            out_specs=[whole(out)] * s.chan + [whole(kept_shape)],
            scratch_shapes=[pltpu.VMEM(out.shape, f32)],
        ),
        out_shape=[out] * s.chan + [kept_shape],
        cost_estimate=cost(1e8, *modes, *modes, *[kept_shape] * 8),
        name="unmix" if adjoint else "mix",
    )(me, *modes, spec_weight)
    return results[:s.chan], results[s.chan]


def weight_kernel(s, width, spec_ref, grad_ref, out_ref):
    for i in range(width):
        for a in range(s.flat // LANES):
            at = slice(a * LANES, (a + 1) * LANES)
            real = spec_ref[0, i, :, at]
            imag = spec_ref[1, i, :, at]
            for o in range(s.ch):
                g_real = grad_ref[0, o, :, at]
                g_imag = grad_ref[1, o, :, at]
                out_ref[0, i, o, :, at] = real * g_real + imag * g_imag
                out_ref[1, i, o, :, at] = real * g_imag - imag * g_real


def weight_grads(s, spec, grad, mode_chunk, total):
    count = s.jl // MODE_CHUNKS
    width = 2
    aliased = [] if total is None else [total]

    def body(spec_ref, grad_ref, *refs):
        weight_kernel(s, width, spec_ref, grad_ref, refs[-1])

    shape = jax.ShapeDtypeStruct((2, s.ch, s.ch, s.jl, s.flat), f32)
    return pl.pallas_call(
        body,
        grid=(s.ch // width,),
        in_specs=[pl.BlockSpec((2, width, count, s.flat), lambda i: (0, i, 0, 0)), whole(grad)]
        + [pl.BlockSpec(memory_space=pl.ANY)] * len(aliased),
        out_specs=pl.BlockSpec((2, width, s.ch, count, s.flat), lambda i: (0, i, 0, mode_chunk, 0)),
        out_shape=shape,
        input_output_aliases={2 + i: i for i in range(len(aliased))},
        cost_estimate=cost(1e8, shape),
        name="weight_grads",
    )(spec, grad, *aliased)


def over_owners(s, p, c, value):
    if p == 0 and c == 0:
        return value
    pairs = [(i, i ^ (p * s.chan + c)) for i in range(s.owners)]
    return lax.ppermute(value, ("planes", "chan"), pairs)


def turns(chan):
    return ((0, 2), (1, 2)) if chan > 2 else ((0, 1), (1, 1))


def over_chan(s, values):
    moved = [values[0]]
    for d in range(1, s.chan):
        moved.append(lax.ppermute(values[d], "chan", [(i, i ^ d) for i in range(s.chan)]))
    return moved


def mode_side(s, sent, tables, spec_weight, adjoint, after):
    mode_chunks = range(MODE_CHUNKS)
    arrived = [over_owners(s, p, c, sent[c][p]) for p, c in distances(s)]
    owned = []
    for m in mode_chunks:
        sent_on = first_pass(s, arrived, tables[0], m, after)
        after = sent_on[:1]
        owned.append(over_chan(s, sent_on))
    mixed = [mix(s, owned[m], spec_weight, m, adjoint) for m in mode_chunks]
    returned = [over_chan(s, v[0]) for v in mixed]
    totals = ()
    for m in mode_chunks:
        totals = first_inverse(s, returned[m], tables[1], m, totals)
    back = {d: over_owners(s, *d, value) for d, value in zip(distances(s), totals)}
    return back, [v[1] for v in mixed]


def fast_local(s, field, cotangent, spec_weight, point_weight, bias):
    second = second_tables(s)
    third = third_tables(s)
    first = first_tables(s)
    halves = [range(k, k + s.chan // 2) for k in (0, s.chan // 2)]
    sent, after = [None] * s.chan, ()
    for start, step in turns(s.chan):
        parts = analysis(s, field, start, step, second, third, after)
        after = parts[0][:1]
        for k, part in enumerate(parts):
            sent[start + k * step] = part
    point = pointwise(field, point_weight, bias)
    back, spec_kept = mode_side(s, sent, first, spec_weight, False, (point,))
    totals, sent = (), []
    for half in halves:
        modes = [back[p, c] for c in half for p in range(s.planes)]
        totals, parts = middle(s, modes, point, cotangent, half[0], second, third, totals)
        sent += parts
    output, grad = totals
    local_grad = pointwise(grad, point_weight.T, jnp.zeros_like(bias))
    back, grad_kept = mode_side(s, sent, first, spec_weight, True, (local_grad,))
    weight_grad = None
    for m in range(MODE_CHUNKS):
        weight_grad = weight_grads(
            s, spec_kept[m], grad_kept[m], m, weight_grad
        )
    totals = ()
    for half in halves:
        modes = [back[p, c] for c in half for p in range(s.planes)]
        totals = final(s, modes, local_grad, half[0], second, third, totals)
    return output, totals[0], weight_grad


def local(field, cotangent, spec_weight, point_weight, bias):
    s = Sizes(field, spec_weight)
    if s.fits():
        return fast_local(s, field, cotangent, spec_weight, point_weight, bias)
    return plain_local(s, field, cotangent, spec_weight, point_weight, bias)


def solution(mesh):
    in_specs = (
        P("groups", None, ("planes", "chan"), None, None),
        P("groups", None, ("planes", "chan"), None, None),
        P(None, None, None, "planes", "chan"),
        P(),
        P(),
    )
    out_specs = (
        P("groups", None, ("planes", "chan"), None, None),
        P("groups", None, ("planes", "chan"), None, None),
        P("groups", None, None, "planes", "chan"),
    )
    return jax.shard_map(local, mesh=mesh, in_specs=in_specs, out_specs=out_specs, check_vma=False)
```

```python
import functools
import math

import numpy as np

import jax
import jax.numpy as jnp
from jax import lax
from jax.experimental import pallas as pl
from jax.experimental.pallas import tpu as pltpu
from jax.sharding import PartitionSpec as P


exact_mode = lax.Precision.HIGHEST


def retained(s, length):
    indices = jnp.arange(2 * s.modes)
    return jnp.where(indices < s.modes, indices, length - 2 * s.modes + indices)


def phase_table(positions, freqs, length):
    turn_count = positions[:, None] * freqs[None, :] % length
    angles = turn_count.astype(jnp.float32) * (2.0 * math.pi / length)
    return (jnp.cos(angles), jnp.sin(angles))


def plain_analysis(s, field):
    batch_size, channels, local_planes, second_length, third_length = field.shape
    plane_count = lax.axis_size("planes")
    channel_groups = lax.axis_size("chan")
    group_width = channels // channel_groups
    local_modes = 2 * s.modes // plane_count
    first_length = local_planes * plane_count * channel_groups
    cosine, sine_part = phase_table(
        jnp.arange(second_length), retained(s, second_length), second_length
    )
    second_table = jnp.stack([cosine, -sine_part], 1).reshape(
        second_length, 2, plane_count, local_modes
    )
    cosine, sine_part = phase_table(jnp.arange(third_length), jnp.arange(s.modes), third_length)
    third_table = jnp.stack(
        [jnp.stack([cosine, -sine_part], 1), jnp.stack([sine_part, cosine], 1)], 0
    )
    grouped = field.reshape(
        batch_size, channel_groups, group_width, local_planes, second_length, third_length
    )
    second_pass = jnp.einsum("bcdxyz,yspk->bcdxspkz", grouped, second_table, precision=exact_mode)
    spectra = jnp.einsum("bcdxspkz,sztm->bpckxdtm", second_pass, third_table, precision=exact_mode)
    spectra = spectra.reshape(
        batch_size, plane_count * channel_groups, local_modes, local_planes, group_width * 2 * s.modes
    )
    arrived = lax.all_to_all(spectra, ("planes", "chan"), split_axis=1, concat_axis=3, tiled=True)
    positions = jnp.arange(first_length)
    arrived = arrived.reshape(batch_size, local_modes, first_length, group_width, 2, s.modes)
    cosine, sine_part = phase_table(positions, retained(s, first_length), first_length)
    first_table = jnp.stack(
        [jnp.stack([cosine, -sine_part], 1), jnp.stack([sine_part, cosine], 1)], 1
    )
    first_pass = jnp.einsum("bkxdsm,xstf->bkdtfm", arrived, first_table, precision=exact_mode)
    first_pass = first_pass.reshape(batch_size, local_modes, group_width, 2, 2 * s.modes * s.modes)
    return lax.all_to_all(first_pass, "chan", split_axis=4, concat_axis=2, tiled=True)


def plain_synthesis(s, spectrum):
    batch_size, local_modes, channels = (spectrum.shape[0], spectrum.shape[1], spectrum.shape[2])
    plane_count = lax.axis_size("planes")
    channel_groups = lax.axis_size("chan")
    group_width = channels // channel_groups
    local_planes = s.gx // (plane_count * channel_groups)
    gathered = lax.all_to_all(spectrum, "chan", split_axis=2, concat_axis=4, tiled=True)
    gathered = gathered.reshape(batch_size, local_modes, group_width, 2, 2 * s.modes, s.modes)
    cosine, sine_part = phase_table(jnp.arange(s.gx), retained(s, s.gx), s.gx)
    cosine_t = cosine.T
    sine_t = sine_part.T
    first_inverse = jnp.stack(
        [jnp.stack([cosine_t, sine_t], -1), jnp.stack([-sine_t, cosine_t], -1)], 0
    )
    first_pass = jnp.einsum("bkdsfm,sfxt->bkxdtm", gathered, first_inverse, precision=exact_mode)
    first_pass = first_pass.reshape(batch_size, local_modes, s.gx, group_width * 2 * s.modes)
    returned = lax.all_to_all(
        first_pass[:, None], ("planes", "chan"), split_axis=3, concat_axis=1, tiled=True
    )
    returned = returned.reshape(
        batch_size, plane_count, channel_groups, local_modes, local_planes, group_width, 2, s.modes
    )
    source_form = "bpckxdtm"
    cosine, sine_part = phase_table(jnp.arange(s.gz), jnp.arange(s.modes), s.gz)
    cosine_t = cosine.T
    sine_t = sine_part.T
    third_inverse = jnp.stack(
        [jnp.stack([cosine_t, sine_t], 1), jnp.stack([-sine_t, cosine_t], 1)], 0
    )
    depth_pass = jnp.einsum(
        source_form + ",tmuz->bcdxpkuz", returned, third_inverse, precision=exact_mode
    )
    cosine, sine_part = phase_table(jnp.arange(s.gy), retained(s, s.gy), s.gy)
    second_inverse = jnp.stack([cosine.T, -sine_part.T], 0).reshape(2, plane_count, local_modes, s.gy)
    physical = jnp.einsum("bcdxpkuz,upky->bcdxyz", depth_pass, second_inverse, precision=exact_mode)
    return physical.reshape(batch_size, channels, local_planes, s.gy, s.gz)


def mode_weighting(s, mode_count):
    depth_mode = jnp.arange(mode_count) % s.modes
    return jnp.where(depth_mode == 0, 1.0, 2.0).astype(jnp.float32) / float(s.gx * s.gy * s.gz)


def contract(operand, weights):
    return jnp.einsum("bkin,iokn->bkon", operand, weights, precision=exact_mode)


def adjoint(operand, weights):
    return jnp.einsum("bkon,iokn->bkin", operand, weights, precision=exact_mode)


def outer_sum(first_operand, second_operand):
    return jnp.einsum("bkin,bkon->iokn", first_operand, second_operand, precision=exact_mode)


def plain_local(s, field, cotangent, spec_weight, point_weight, bias):
    spectrum = plain_analysis(s, field)
    weight_re = spec_weight[0]
    weight_im = spec_weight[1]
    spec_re = spectrum[:, :, :, 0]
    spec_im = spectrum[:, :, :, 1]
    weighting = mode_weighting(s, spectrum.shape[-1])
    mixed_re = (contract(spec_re, weight_re) - contract(spec_im, weight_im)) * weighting
    mixed_im = (contract(spec_re, weight_im) + contract(spec_im, weight_re)) * weighting
    mixed_modes = jnp.stack([mixed_re, mixed_im], 3)
    spectral = plain_synthesis(s, mixed_modes)
    pointwise = jnp.einsum("bixyz,io->boxyz", field, point_weight, precision=exact_mode)
    preactivation = spectral + pointwise + bias[None, :, None, None, None]
    normal_cdf = 0.5 * (1.0 + lax.erf(preactivation * (1.0 / math.sqrt(2.0))))
    output = preactivation * normal_cdf
    derivative = normal_cdf + preactivation * jnp.exp(-0.5 * preactivation * preactivation) * (
        1.0 / math.sqrt(2.0 * math.pi)
    )
    pre_grad = cotangent * derivative
    raw_grad = plain_analysis(s, pre_grad)
    grad_re = raw_grad[:, :, :, 0] * weighting
    grad_im = raw_grad[:, :, :, 1] * weighting
    spectrum_grad = jnp.stack(
        [
            adjoint(grad_re, weight_re) + adjoint(grad_im, weight_im),
            adjoint(grad_im, weight_re) - adjoint(grad_re, weight_im),
        ],
        3,
    )
    weight_grad = jnp.stack(
        [
            outer_sum(spec_re, grad_re) + outer_sum(spec_im, grad_im),
            outer_sum(spec_re, grad_im) - outer_sum(spec_im, grad_re),
        ],
        0,
    )
    local_grad = jnp.einsum("boxyz,io->bixyz", pre_grad, point_weight, precision=exact_mode)
    field_grad = local_grad + plain_synthesis(s, spectrum_grad)
    return (output, field_grad, weight_grad)


LANES = 128
BLOCK = 4
MODE_CHUNKS = 2
f32 = jnp.float32
bf16 = jnp.bfloat16


class Sizes:
    def __init__(self, field, spec_weight):
        self.planes = lax.axis_size("planes")
        self.chan = lax.axis_size("chan")
        self.owners = self.planes * self.chan
        _, self.ch, self.lx, self.gy, self.gz = field.shape
        self.gx = self.lx * self.owners
        _, _, _, self.jl, local_flat = spec_weight.shape
        self.jy = self.jl * self.planes
        self.flat = local_flat
        self.modes = self.jy // 2
        self.jxl = local_flat // self.modes
        self.jx = self.jxl * self.chan
        self.gw = self.ch // self.chan
        self.scale = 1.0 / float(self.gx * self.gy * self.gz)

    def fits(self):
        return (
            self.gw == 4
            and self.gw * self.modes == LANES
            and self.gz == LANES
            and self.gy == LANES
            and self.jy * 2 == LANES
            and self.jx * 2 == LANES
            and self.flat % LANES == 0
            and self.ch * 16 == 2 * LANES
            and self.jl % (8 * MODE_CHUNKS) == 0
            and self.lx % (2 * BLOCK) == 0
            and self.gx == LANES
            and self.chan & (self.chan - 1) == 0
            and self.planes & (self.planes - 1) == 0
        )


def kept(count, length):
    index = np.arange(count)
    return np.where(index < count // 2, index, length - count + index)


def waves(freqs, length):
    turns = (freqs[:, None] * np.arange(length)[None, :]) % length
    angles = turns * (2.0 * math.pi / length)
    return np.cos(angles), np.sin(angles)


def two_terms(table):
    table = np.asarray(table, np.float32)
    high = table.astype(jnp.bfloat16)
    low = (table - high.astype(np.float32)).astype(jnp.bfloat16)
    return high, low


def stacked(table):
    return np.concatenate(two_terms(table), 0)


def second_tables(s):
    cosine, sine = waves(kept(s.jy, s.gy), s.gy)
    forward = np.concatenate([cosine, sine], 0)
    inverse = np.concatenate(
        [np.concatenate([cosine.T, -sine.T], 1), np.concatenate([sine.T, cosine.T], 1)], 0
    )
    return stacked(forward), stacked(inverse)


def third_tables(s):
    cosine, sine = waves(np.arange(s.modes), s.gz)
    table = np.zeros((2, s.gz, 2, 2, s.modes))
    for c in range(2):
        table[c, :, 0, c] = cosine.T
        table[c, :, 1, c] = -sine.T
    table = table.reshape(2 * s.gz, LANES)
    forward = np.concatenate(two_terms(table), 1)
    high, low = two_terms(table.T)
    return forward, np.concatenate([high, low], 1)


def first_tables(s):
    cosine, sine = waves(kept(s.jx, s.gx), s.gx)
    c4 = cosine.reshape(s.chan, s.jxl, s.owners, s.lx)
    s4 = sine.reshape(s.chan, s.jxl, s.owners, s.lx)
    forward = np.zeros((s.chan, 2, s.jxl, s.owners, 2, s.lx))
    inverse = np.zeros((s.owners, 2, s.lx, s.chan, 2, s.jxl))
    for out, inp, sign, wave in ((0, 0, 1, c4), (0, 1, 1, s4), (1, 0, -1, s4), (1, 1, 1, c4)):
        forward[:, out, :, :, inp] = sign * wave
        inverse[:, inp, :, :, out] = sign * wave.transpose(2, 3, 0, 1)
    rows = s.chan * 2 * s.jxl
    return forward.reshape(rows, -1), inverse.reshape(-1, rows)


def terms(value):
    high = value.astype(bf16)
    return high, (value - high.astype(f32)).astype(bf16)


def dot(a, b):
    return jnp.dot(a, b, preferred_element_type=f32)


def square_dot(table, value):
    high, low = terms(value)
    both = dot(jnp.concatenate([table, table], 1), jnp.concatenate([high, low], 0))
    half = both.shape[0] // 2
    return both[:half] + both[half:]


def gelu_parts(v):
    normal_cdf = 0.5 * (1.0 + lax.erf(v * (1.0 / math.sqrt(2.0))))
    slope = normal_cdf + v * jnp.exp(-0.5 * v * v) * (1.0 / math.sqrt(2.0 * math.pi))
    return normal_cdf, slope


def half_lanes(shape):
    return lax.broadcasted_iota(jnp.int32, shape, 1) < LANES // 2


def place_terms(s, row, value, split):
    half = split.shape[0] // 2
    high, low = terms(value)
    split[pl.ds(pl.multiple_of(row * s.gy, s.gy), s.gy), :] = high
    split[pl.ds(pl.multiple_of(half + row * s.gy, s.gy), s.gy), :] = low


def forward_planes(s, split, third_ref, second_ref, held):
    half = split.shape[0] // 2
    both = dot(split[...], third_ref[...])
    deep = both[:half, :LANES] + both[:half, LANES:] + both[half:, :LANES]
    first = half_lanes((s.jy, LANES))
    for x in range(BLOCK):
        side = [deep[(2 * x + q) * s.gy:(2 * x + q + 1) * s.gy] for q in range(2)]
        out = square_dot(second_ref[...], jnp.concatenate(side, 1))
        pairs = []
        for k in range(2):
            turned = pltpu.roll(out[s.jy:, k * LANES:(k + 1) * LANES], LANES // 2, 1)
            pairs.append(out[:s.jy, k * LANES:(k + 1) * LANES] + jnp.where(first, turned, -turned))
        rows = slice(x * s.jy, (x + 1) * s.jy)
        held[rows, :LANES] = jnp.where(first, pairs[0], pltpu.roll(pairs[1], LANES // 2, 1))
        held[rows, LANES:] = jnp.where(first, pltpu.roll(pairs[0], LANES // 2, 1), pairs[1])


def scatter_modes(s, outs, held):
    me = lax.axis_index("planes")
    first = pl.program_id(1) * BLOCK
    for k, group in enumerate(outs):

        @pl.when(pl.program_id(0) == k)
        def _(group=group):
            for d, out_ref in enumerate(group):
                for x in range(BLOCK):
                    at = pl.ds(pl.multiple_of(x * s.jy + (me ^ d) * s.jl, s.jl), s.jl)
                    for part in range(2):
                        rows = pl.ds(part * s.lx + first + x, s.jl, stride=2 * s.lx)
                        out_ref[rows, :] = held[at, part * LANES:(part + 1) * LANES]


def gather_modes(s, ins, gathered):
    me = lax.axis_index("planes")
    first = pl.program_id(1) * BLOCK
    for k, group in enumerate(ins):

        @pl.when(pl.program_id(0) == k)
        def _(group=group):
            for d, in_ref in enumerate(group):
                for x in range(BLOCK):
                    for part in range(2):
                        at = pl.ds(pl.multiple_of(part * s.jy + (me ^ d) * s.jl, s.jl), s.jl)
                        rows = pl.ds(part * s.lx + first + x, s.jl, stride=2 * s.lx)
                        gathered[x // 2, at, (x % 2) * LANES:(x % 2 + 1) * LANES] = in_ref[rows, :]


def by_group(s, refs):
    return [refs[k:k + s.planes] for k in range(0, len(refs), s.planes)]


def inverse_planes(s, gathered, second_ref, third_ref, planes):
    first = half_lanes((s.gy, LANES))
    sides = []
    for step in range(BLOCK // 2):
        out = square_dot(second_ref[...], gathered[step])
        for k in range(2):
            real = out[:s.gy, k * LANES:(k + 1) * LANES]
            imag = out[s.gy:, k * LANES:(k + 1) * LANES]
            for side in (
                jnp.where(first, real, pltpu.roll(imag, LANES // 2, 1)),
                jnp.where(first, pltpu.roll(real, LANES // 2, 1), imag),
            ):
                high, low = terms(side)
                sides.append(jnp.concatenate([high, low], 1))
    table = third_ref[...]
    both = dot(jnp.concatenate(sides, 0), jnp.concatenate([table, table], 0))
    planes[...] = both[:, :2 * s.gz] + both[:, 2 * s.gz:]


def plane_rows(s, row):
    return pl.ds(pl.multiple_of(row * s.gy, s.gy), s.gy)


def analysis_kernel(s, field_ref, third_ref, second_ref, outs, split, held):
    for x in range(BLOCK):
        for q in range(2):
            tile = jnp.concatenate([field_ref[0, 2 * q, x], field_ref[0, 2 * q + 1, x]], 1)
            place_terms(s, 2 * x + q, tile, split)
    forward_planes(s, split, third_ref, second_ref, held)
    scatter_modes(s, outs, held)


def middle_kernel(
    s, ins, point_ref, cot_ref, inv_second, inv_third, third_ref, second_ref,
    output_ref, grad_ref, outs, gathered, planes, split, held,
):
    gather_modes(s, ins, gathered)
    inverse_planes(s, gathered, inv_second, inv_third, planes)

    def one(x, carry):
        for q in range(2):
            grads = []
            for c in range(2):
                v = planes[plane_rows(s, 2 * x + q), c * s.gz:(c + 1) * s.gz] + point_ref[0, 2 * q + c, x]
                normal_cdf, slope = gelu_parts(v)
                output_ref[0, 2 * q + c, x] = v * normal_cdf
                grad = cot_ref[0, 2 * q + c, x] * slope
                grad_ref[0, 2 * q + c, x] = grad
                grads.append(grad)
            place_terms(s, 2 * x + q, jnp.concatenate(grads, 1), split)
        return carry

    lax.fori_loop(0, BLOCK, one, 0)
    forward_planes(s, split, third_ref, second_ref, held)
    scatter_modes(s, outs, held)


def final_kernel(s, ins, local_ref, inv_second, inv_third, out_ref, gathered, planes):
    gather_modes(s, ins, gathered)
    inverse_planes(s, gathered, inv_second, inv_third, planes)

    def one(x, carry):
        for q in range(2):
            for c in range(2):
                out_ref[0, 2 * q + c, x] = (
                    planes[plane_rows(s, 2 * x + q), c * s.gz:(c + 1) * s.gz] + local_ref[0, 2 * q + c, x]
                )
        return carry

    lax.fori_loop(0, BLOCK, one, 0)


def whole(array):
    rank = len(array.shape)
    return pl.BlockSpec(array.shape, lambda *_: (0,) * rank, pipeline_mode=pl.Buffered(1))


def cost(flops, *arrays):
    count = sum(int(np.prod(a.shape)) * a.dtype.itemsize for a in arrays)
    return pl.CostEstimate(flops=int(flops), bytes_accessed=count, transcendentals=0)


def anywhere():
    return pl.BlockSpec(memory_space=pl.ANY)


def chan_index():
    return lax.axis_index("chan").astype(jnp.int32).reshape(1)


def grid_spec(s, start, step=1):
    return pl.BlockSpec(
        (1, s.gw, BLOCK, s.gy, s.gz), lambda k, x, me: (0, me[0] ^ (start + step * k), x, 0, 0)
    )


def mode_shape(s):
    return jax.ShapeDtypeStruct((s.jl * 2 * s.lx, LANES), f32)


def forward_scratch(s):
    return [
        pltpu.VMEM((2 * BLOCK * 2 * s.gy, 2 * s.gz), bf16),
        pltpu.VMEM((BLOCK * s.jy, 2 * LANES), f32),
    ]


def inverse_scratch(s):
    return [
        pltpu.VMEM((BLOCK // 2, 2 * s.jy, 2 * LANES), f32),
        pltpu.VMEM((BLOCK * 2 * s.gy, 2 * s.gz), f32),
    ]


def group_call(s, groups, body, in_specs, out_specs, out_shape, scratch, aliases, estimate, operands):
    return pl.pallas_call(
        body,
        grid_spec=pltpu.PrefetchScalarGridSpec(
            num_scalar_prefetch=1,
            grid=(groups, s.lx // BLOCK),
            in_specs=in_specs,
            out_specs=out_specs,
            scratch_shapes=scratch,
        ),
        out_shape=out_shape,
        input_output_aliases=aliases,
        cost_estimate=estimate,
    )(chan_index(), *operands)


def analysis(s, field, start, step, second, third, after):
    tables = (third[0], second[0])
    out = mode_shape(s)
    count = 1 + len(tables)

    def body(me_ref, *refs):
        outs = by_group(s, refs[count + len(after):-2])
        analysis_kernel(s, *refs[:count], outs, *refs[-2:])

    return by_group(s, group_call(
        s, s.chan // 2, body,
        [grid_spec(s, start, step)] + [whole(t) for t in tables] + [anywhere()] * len(after),
        [whole(out)] * (s.owners // 2),
        [out] * (s.owners // 2),
        forward_scratch(s),
        {},
        cost(3e9, *[out] * 40),
        (field, *tables, *after),
    ))


def middle(s, modes, point, cotangent, start, second, third, totals):
    tables = (second[1], third[1], third[0], second[0])
    out = mode_shape(s)
    spec = grid_spec(s, start)
    sources = len(modes)
    count = sources + 2 + len(tables)

    def body(me_ref, *refs):
        rest = refs[count + len(totals):]
        middle_kernel(
            s, by_group(s, refs[:sources]), *refs[sources:count], rest[0], rest[1],
            by_group(s, rest[2:-4]), *rest[-4:],
        )

    grid = jax.ShapeDtypeStruct(point.shape, f32)
    results = group_call(
        s, sources // s.planes, body,
        [whole(out)] * sources + [spec, spec] + [whole(t) for t in tables] + [anywhere()] * len(totals),
        [spec, spec] + [whole(out)] * sources,
        [grid, grid] + [out] * sources,
        inverse_scratch(s) + forward_scratch(s),
        {1 + count + i: i for i in range(len(totals))},
        cost(6e9, *[out] * 144),
        (*modes, point, cotangent, *tables, *totals),
    )
    return results[:2], by_group(s, results[2:])


def final(s, modes, local_grad, start, second, third, totals):
    tables = (second[1], third[1])
    out = mode_shape(s)
    spec = grid_spec(s, start)
    sources = len(modes)
    count = sources + 1 + len(tables)

    def body(me_ref, *refs):
        final_kernel(s, by_group(s, refs[:sources]), *refs[sources:count], *refs[count + len(totals):])

    return group_call(
        s, sources // s.planes, body,
        [whole(out)] * sources + [spec] + [whole(t) for t in tables] + [anywhere()] * len(totals),
        [spec],
        [jax.ShapeDtypeStruct(local_grad.shape, f32)],
        inverse_scratch(s),
        {1 + count + i: i for i in range(len(totals))},
        cost(3e9, *[out] * 72),
        (*modes, local_grad, *tables, *totals),
    )


def pointwise_kernel(values_ref, mixing_ref, bias_ref, out_ref):
    channels, strip = values_ref.shape[1], mixing_ref.shape[1] // values_ref.shape[1]
    rows = channels * strip

    def strips(step, carry):
        at = [pl.ds(pl.multiple_of((2 * step + k) * strip, strip), strip) for k in range(2)]
        value = jnp.concatenate([values_ref[0, :, 0, a, :].reshape(rows, LANES) for a in at], 1)
        high, low = terms(value)
        both = dot(mixing_ref[...], high)
        out = both[:rows] + both[rows:] + dot(mixing_ref[:rows, :], low)
        for k in range(2):
            one = out[:, k * LANES:(k + 1) * LANES] + bias_ref[...]
            out_ref[0, :, 0, at[k], :] = one.reshape(channels, strip, LANES)
        return carry

    lax.fori_loop(0, values_ref.shape[3] // (2 * strip), strips, 0, unroll=True)


def pointwise(values, weight, bias):
    _, channels, lx, gy, gz = values.shape
    strip = 2 * LANES // channels
    rows = channels * strip
    spread = np.repeat(np.eye(channels, dtype=np.float32), strip, 0)
    diagonal = np.tile(np.eye(strip, dtype=bool), (channels, channels))
    exact = functools.partial(jnp.dot, precision=lax.Precision.HIGHEST)
    mixing = jnp.where(diagonal, exact(exact(spread, weight.T), spread.T), 0.0)
    high = lax.reduce_precision(mixing, 8, 7)
    mixing = jnp.concatenate([high.astype(bf16), (mixing - high).astype(bf16)], 0)
    bias_rows = jnp.broadcast_to(exact(spread, bias[:, None]), (rows, LANES))
    spec = pl.BlockSpec((1, channels, 1, gy, gz), lambda x: (0, 0, x, 0, 0))
    return pl.pallas_call(
        pointwise_kernel,
        grid=(lx,),
        in_specs=[spec, whole(mixing), whole(bias_rows)],
        out_specs=spec,
        out_shape=jax.ShapeDtypeStruct(values.shape, f32),
        cost_estimate=cost(6e9, values, values),
        name="pointwise",
    )(values, mixing, bias_rows)


def distances(s):
    return [(p, c) for p in range(s.planes) for c in range(s.chan)]


def owner_rows(s, p, c, step):
    owner = (lax.axis_index("planes") ^ p) * s.chan + (lax.axis_index("chan") ^ c)
    return pl.ds(pl.multiple_of(owner * step, step), step)


def first_kernel(s, ins, stacked_ref, outs, gathered, held):
    me = lax.axis_index("chan")
    rows = held.shape[1]
    per = 2 * s.lx
    step = rows // len(outs)
    for pair in range(gathered.shape[0]):
        for in_ref, (p, c) in zip(ins, distances(s)):
            for j in range(2):
                start = (2 * pair + j) * per
                gathered[pair, owner_rows(s, p, c, per), j * LANES:(j + 1) * LANES] = in_ref[start:start + per, :]
        high, low = terms(gathered[pair])
        both = dot(stacked_ref[...], high)
        held[pair] = both[:rows] + both[rows:] + dot(stacked_ref[:rows, :], low)
        for d, out_ref in enumerate(outs):
            at = pl.ds(pl.multiple_of((me ^ d) * step, step), step)
            for j in range(2):
                start = (2 * pair + j) * step
                out_ref[start:start + step, :] = held[pair, at, j * LANES:(j + 1) * LANES]


def first_pass(s, arrived, table, mode_chunk, after):
    rows = table.shape[0]
    tall = stacked(table)
    pairs = s.jl // MODE_CHUNKS // 2
    out = jax.ShapeDtypeStruct((pairs * 2 * 2 * s.jxl, LANES), f32)

    def body(*refs):
        outs = refs[s.owners + 1 + len(after):-2]
        first_kernel(s, refs[:s.owners], refs[s.owners], outs, *refs[-2:])

    return pl.pallas_call(
        body,
        grid=(1,),
        in_specs=[
            pl.BlockSpec(
                (pairs * 4 * s.lx, LANES), lambda j: (mode_chunk, 0), pipeline_mode=pl.Buffered(1)
            )
        ] * s.owners
        + [whole(tall)]
        + [anywhere()] * len(after),
        out_specs=[whole(out)] * s.chan,
        out_shape=[out] * s.chan,
        scratch_shapes=[
            pltpu.VMEM((pairs, s.owners * 2 * s.lx, 2 * LANES), f32),
            pltpu.VMEM((pairs, rows, 2 * LANES), f32),
        ],
        cost_estimate=cost(1e9 / MODE_CHUNKS, *[out] * 12),
        name="first_forward",
    )(*arrived, tall, *after)


def back_kernel(s, ins, table_ref, outs, gathered, held):
    me = lax.axis_index("chan")
    step = 2 * s.jxl
    per = 2 * s.lx
    for pair in range(gathered.shape[0]):
        for d, in_ref in enumerate(ins):
            at = pl.ds(pl.multiple_of((me ^ d) * step, step), step)
            for j in range(2):
                start = (2 * pair + j) * step
                gathered[pair, at, j * LANES:(j + 1) * LANES] = in_ref[start:start + step, :]
        held[pair] = square_dot(table_ref[...], gathered[pair])
        for out_ref, (p, c) in zip(outs, distances(s)):
            for j in range(2):
                start = (2 * pair + j) * per
                out_ref[start:start + per, :] = held[pair, owner_rows(s, p, c, per), j * LANES:(j + 1) * LANES]


def first_inverse(s, modes, table, mode_chunk, totals):
    square = stacked(table)
    pairs = s.jl // MODE_CHUNKS // 2
    out = mode_shape(s)
    count = s.chan + 1

    def body(*refs):
        back_kernel(s, refs[:s.chan], refs[s.chan], refs[count + len(totals):-2], *refs[-2:])

    return pl.pallas_call(
        body,
        grid=(1,),
        in_specs=[whole(v) for v in modes]
        + [whole(square)]
        + [anywhere()] * len(totals),
        out_specs=[
            pl.BlockSpec(
                (pairs * 4 * s.lx, LANES), lambda j: (mode_chunk, 0), pipeline_mode=pl.Buffered(1)
            )
        ] * s.owners,
        out_shape=[out] * s.owners,
        scratch_shapes=[
            pltpu.VMEM((pairs, s.chan * 2 * s.jxl, 2 * LANES), f32),
            pltpu.VMEM((pairs, s.owners * 2 * s.lx, 2 * LANES), f32),
        ],
        input_output_aliases={count + i: i for i in range(len(totals))},
        cost_estimate=cost(1e9 / MODE_CHUNKS, *modes, *modes, *modes),
        name="first_inverse",
    )(*modes, square, *totals)


def swap_groups(pieces, width):
    count = len(pieces)
    lane = lax.broadcasted_iota(jnp.int32, pieces[0].shape, 1)
    step = count // 2
    pieces = list(pieces)
    while step:
        upper = (lane // (width * step)) % 2 == 1
        for a in range(count):
            if a & step:
                continue
            low, high = pieces[a], pieces[a + step]
            pieces[a] = jnp.where(upper, pltpu.roll(high, width * step, 1), low)
            pieces[a + step] = jnp.where(upper, high, pltpu.roll(low, LANES - width * step, 1))
        step //= 2
    return pieces


def spread_modes(s, count, ins, out_ref, factor=None):
    stride = 2 * s.jxl
    me = lax.axis_index("chan")

    def one(a, carry):
        at = pl.ds(pl.multiple_of(a * LANES, LANES), LANES)
        for d, in_ref in enumerate(ins):
            for part in range(2):
                pieces = [
                    in_ref[pl.ds(part * s.jxl + a * s.gw + b, count, stride=stride), :]
                    for b in range(s.gw)
                ]
                for c, piece in enumerate(swap_groups(pieces, s.modes)):
                    if factor is not None:
                        piece = piece * factor
                    out_ref[part, (me ^ d) * s.gw + c, :, at] = piece
        return carry

    lax.fori_loop(0, s.jxl // s.gw, one, 0)


def depth_factor(s, shape):
    lane = lax.broadcasted_iota(jnp.int32, shape, 1)
    return jnp.where(lane % s.modes == 0, s.scale, 2.0 * s.scale).astype(f32)


def store_block(s, count, block, outs, held):
    stride = 2 * s.jxl
    for part in range(2):
        for a in range(s.flat // LANES):
            for b, piece in enumerate(swap_groups([block[part][c][a] for c in range(s.gw)], s.modes)):
                held[pl.ds(part * s.jxl + a * s.gw + b, count, stride=stride), :] = piece
    for d, out_ref in enumerate(outs):

        @pl.when(pl.program_id(0) == d)
        def _(out_ref=out_ref):
            out_ref[...] = held[...]


def mix_kernel(s, count, adjoint, *refs):
    ins, weight_ref, outs = refs[1:1 + s.chan], refs[1 + s.chan], refs[2 + s.chan:2 + 2 * s.chan]
    kept_ref, held = refs[-2:]
    factor = depth_factor(s, (count, LANES))

    @pl.when(pl.program_id(0) == 0)
    def _():
        spread_modes(s, count, ins, kept_ref, factor if adjoint else None)

    pieces = s.flat // LANES
    block = [[[None] * pieces for _ in range(s.gw)] for _ in range(2)]
    for a in range(pieces):
        at = slice(a * LANES, (a + 1) * LANES)
        reals = [None] * s.gw
        imags = [None] * s.gw
        for i in range(s.ch):
            real = kept_ref[0, i, :, at]
            imag = kept_ref[1, i, :, at]
            for o in range(s.gw):
                pick = (o, i) if adjoint else (i, o)
                w_real = weight_ref[(0,) + pick + (slice(None), at)]
                w_imag = weight_ref[(1,) + pick + (slice(None), at)]
                if adjoint:
                    new_real = real * w_real + imag * w_imag
                    new_imag = imag * w_real - real * w_imag
                else:
                    new_real = real * w_real - imag * w_imag
                    new_imag = real * w_imag + imag * w_real
                reals[o] = new_real if i == 0 else reals[o] + new_real
                imags[o] = new_imag if i == 0 else imags[o] + new_imag
        for o in range(s.gw):
            block[0][o][a] = reals[o] if adjoint else reals[o] * factor
            block[1][o][a] = imags[o] if adjoint else imags[o] * factor
    store_block(s, count, block, outs, held)


def mix(s, modes, spec_weight, mode_chunk, adjoint):
    count = s.jl // MODE_CHUNKS
    kept_shape = jax.ShapeDtypeStruct((2, s.ch, count, s.flat), f32)
    me = chan_index()
    if adjoint:
        weights = pl.BlockSpec((2, s.gw, s.ch, count, s.flat), lambda d, me: (0, d ^ me[0], 0, mode_chunk, 0))
    else:
        weights = pl.BlockSpec((2, s.ch, s.gw, count, s.flat), lambda d, me: (0, 0, d ^ me[0], mode_chunk, 0))
    out = jax.ShapeDtypeStruct(modes[0].shape, f32)
    results = pl.pallas_call(
        functools.partial(mix_kernel, s, count, adjoint),
        grid_spec=pltpu.PrefetchScalarGridSpec(
            num_scalar_prefetch=1,
            grid=(s.chan,),
            in_specs=[whole(v) for v in modes] + [weights],
            out_specs=[whole(out)] * s.chan + [whole(kept_shape)],
            scratch_shapes=[pltpu.VMEM(out.shape, f32)],
        ),
        out_shape=[out] * s.chan + [kept_shape],
        cost_estimate=cost(1e8, *modes, *modes, *[kept_shape] * 8),
        name="unmix" if adjoint else "mix",
    )(me, *modes, spec_weight)
    return results[:s.chan], results[s.chan]


def weight_kernel(s, width, spec_ref, grad_ref, out_ref):
    for i in range(width):
        for a in range(s.flat // LANES):
            at = slice(a * LANES, (a + 1) * LANES)
            real = spec_ref[0, i, :, at]
            imag = spec_ref[1, i, :, at]
            for o in range(s.ch):
                g_real = grad_ref[0, o, :, at]
                g_imag = grad_ref[1, o, :, at]
                out_ref[0, i, o, :, at] = real * g_real + imag * g_imag
                out_ref[1, i, o, :, at] = real * g_imag - imag * g_real


def weight_grads(s, spec, grad, mode_chunk, total):
    count = s.jl // MODE_CHUNKS
    width = 2
    aliased = [] if total is None else [total]

    def body(spec_ref, grad_ref, *refs):
        weight_kernel(s, width, spec_ref, grad_ref, refs[-1])

    shape = jax.ShapeDtypeStruct((2, s.ch, s.ch, s.jl, s.flat), f32)
    return pl.pallas_call(
        body,
        grid=(s.ch // width,),
        in_specs=[pl.BlockSpec((2, width, count, s.flat), lambda i: (0, i, 0, 0)), whole(grad)]
        + [pl.BlockSpec(memory_space=pl.ANY)] * len(aliased),
        out_specs=pl.BlockSpec((2, width, s.ch, count, s.flat), lambda i: (0, i, 0, mode_chunk, 0)),
        out_shape=shape,
        input_output_aliases={2 + i: i for i in range(len(aliased))},
        cost_estimate=cost(1e8, shape),
        name="weight_grads",
    )(spec, grad, *aliased)


def over_owners(s, p, c, value):
    if p == 0 and c == 0:
        return value
    pairs = [(i, i ^ (p * s.chan + c)) for i in range(s.owners)]
    return lax.ppermute(value, ("planes", "chan"), pairs)


def turns(chan):
    return ((0, 2), (1, 2)) if chan > 2 else ((0, 1), (1, 1))


def over_chan(s, values):
    moved = [values[0]]
    for d in range(1, s.chan):
        moved.append(lax.ppermute(values[d], "chan", [(i, i ^ d) for i in range(s.chan)]))
    return moved


def mode_side(s, sent, tables, spec_weight, adjoint, after):
    mode_chunks = range(MODE_CHUNKS)
    arrived = [over_owners(s, p, c, sent[c][p]) for p, c in distances(s)]
    owned, mixed, returned = [], [], []
    for m in mode_chunks:
        sent_on = first_pass(s, arrived, tables[0], m, after)
        after = sent_on[:1]
        owned.append(over_chan(s, sent_on))
    for m in mode_chunks:
        mixed.append(mix(s, owned[m], spec_weight, m, adjoint))
        returned.append(over_chan(s, mixed[m][0]))
    totals = ()
    for m in mode_chunks:
        totals = first_inverse(s, returned[m], tables[1], m, totals)
    back = {d: over_owners(s, *d, value) for d, value in zip(distances(s), totals)}
    return back, [v[1] for v in mixed]


def fast_local(s, field, cotangent, spec_weight, point_weight, bias):
    second = second_tables(s)
    third = third_tables(s)
    first = first_tables(s)
    halves = [range(k, k + s.chan // 2) for k in (0, s.chan // 2)]
    sent, after = [None] * s.chan, ()
    for start, step in turns(s.chan):
        parts = analysis(s, field, start, step, second, third, after)
        after = parts[0][:1]
        for k, part in enumerate(parts):
            sent[start + k * step] = part
    point = pointwise(field, point_weight, bias)
    back, spec_kept = mode_side(s, sent, first, spec_weight, False, (point,))
    totals, sent = (), []
    for half in halves:
        modes = [back[p, c] for c in half for p in range(s.planes)]
        totals, parts = middle(s, modes, point, cotangent, half[0], second, third, totals)
        sent += parts
    output, grad = totals
    local_grad = pointwise(grad, point_weight.T, jnp.zeros_like(bias))
    back, grad_kept = mode_side(s, sent, first, spec_weight, True, (local_grad,))
    weight_grad = None
    for m in range(MODE_CHUNKS):
        weight_grad = weight_grads(
            s, spec_kept[m], grad_kept[m], m, weight_grad
        )
    totals = ()
    for half in halves:
        modes = [back[p, c] for c in half for p in range(s.planes)]
        totals = final(s, modes, local_grad, half[0], second, third, totals)
    return output, totals[0], weight_grad


def local(field, cotangent, spec_weight, point_weight, bias):
    s = Sizes(field, spec_weight)
    if s.fits():
        return fast_local(s, field, cotangent, spec_weight, point_weight, bias)
    return plain_local(s, field, cotangent, spec_weight, point_weight, bias)


def solution(mesh):
    in_specs = (
        P("groups", None, ("planes", "chan"), None, None),
        P("groups", None, ("planes", "chan"), None, None),
        P(None, None, None, "planes", "chan"),
        P(),
        P(),
    )
    out_specs = (
        P("groups", None, ("planes", "chan"), None, None),
        P("groups", None, ("planes", "chan"), None, None),
        P("groups", None, None, "planes", "chan"),
    )
    return jax.shard_map(local, mesh=mesh, in_specs=in_specs, out_specs=out_specs, check_vma=False)
```
